32 devices in a mesh: dp: 8 (over y, x, core), mp: 4 (over z).
Axes of the slice: x: 2, y: 2, z: 4, core: 2. Of those that a mesh axis runs over, the one named last changes fastest.
Arguments:
- features: bfloat16 [16384, 2048], P('dp', 'mp'), may hold values from -6 to 6
- neighbour_lists: int32 [16384, 32], P('dp'), may hold values from -1 to 2047, as said below
- node_counts: int32 [8], P('dp'), may hold values from 1024 to 2048, as said below
- weight: bfloat16 [2048, 2048], P(None, 'mp'), may hold values from -0.375 to 0.375
- bias_terms: bfloat16 [2048], P('mp'), may hold values from -1.796875 to 1.796875
- cotangent: bfloat16 [16384, 2048], P('dp', 'mp'), may hold values from -6 to 6
Outputs:
- output: bfloat16 [16384, 2048], P('dp', 'mp')
- features_grad: bfloat16 [16384, 2048], P('dp', 'mp')
- weight_grad: float32 [2048, 2048], P(None, 'mp')
- bias_grad: float32 [2048], P('mp')
The draws below stay inside these ranges and needn't reach their ends.
Inputs may be any that keep to these rules, and one draw needn't show every extreme that they name: `node_counts`: in every draw some group holds exactly 2048 true nodes and another exactly half of that. `neighbour_lists`: each row lists its neighbours first and fills the rest with -1. Neighbours are true nodes of the same group and the same cluster, never the row itself, and may repeat; clusters are runs of consecutive slots. Padding rows hold only -1. In every group the first row has 32 neighbours.
All inputs are finite; a program needn't handle non-finite values.
Results may differ from the reference program's by a relative error of at most 0.0064.
Values may be sent and summed in bfloat16 or wider, within the bound.
No kernel may reach another device: no remote copies, remote signals or barrier semaphores. Data moves between devices by JAX's collectives and lax.ppermute only.
A program may use at most 192 MiB of HBM per device.

```python
import jax
import jax.numpy as jnp
from jax import lax

HID = 2048
NODE_DEV = 2048
DEG = 32
MINC = 512
GROUPS = 8
NODES = 16384
N_DP = 8


def group_counts(key):
    draws = jax.random.randint(jax.random.fold_in(key, 11), (GROUPS,), NODE_DEV // 2, NODE_DEV + 1)
    fullest = jax.random.randint(jax.random.fold_in(key, 12), (), 0, GROUPS)
    emptiest = (fullest + 1 + jax.random.randint(jax.random.fold_in(key, 13), (), 0, GROUPS - 1)) % GROUPS
    groups = jnp.arange(GROUPS)
    draws = jnp.where(groups == emptiest, NODE_DEV // 2, draws)
    return jnp.where(groups == fullest, NODE_DEV, draws).astype(jnp.int32)


def draw_node_counts(key, part):
    return group_counts(key)


def draw_neighbour_lists(key, part):
    counts = group_counts(key)
    pieces = NODE_DEV // MINC + 1
    lengths = jax.random.randint(jax.random.fold_in(key, 21), (GROUPS, pieces), MINC, 5 * MINC + 1)
    cuts = jnp.cumsum(lengths, axis=1)
    cuts = jnp.where(cuts > counts[:, None] - MINC, 4 * NODE_DEV, cuts)
    nodes = jnp.arange(NODE_DEV)
    before = jnp.sum((cuts[:, None, :] <= nodes[None, :, None]).astype(jnp.int32), axis=2)
    starts = jnp.where(before > 0, jnp.take_along_axis(cuts, jnp.maximum(before - 1, 0), axis=1), 0)
    ends = jnp.minimum(jnp.take_along_axis(cuts, before, axis=1), counts[:, None])
    spans = jnp.maximum(ends - starts, 1)
    wanted = jax.random.randint(jax.random.fold_in(key, 22), (GROUPS, NODE_DEV), 1, DEG + 1)
    wanted = jnp.where(nodes[None, :] == 0, DEG, wanted)
    degree = jnp.minimum(wanted, spans - 1)
    degree = jnp.where(nodes[None, :] < counts[:, None], degree, 0)
    offsets = jax.random.randint(jax.random.fold_in(key, 23), (GROUPS, NODE_DEV, DEG), 0, 1 << 20)
    places = jnp.arange(DEG)
    forced = (nodes[None, :, None] == NODE_DEV - 2) & (places[None, None, :] == 0)
    offsets = jnp.where(forced, 0, offsets)
    offsets = offsets % jnp.maximum(spans - 1, 1)[:, :, None]
    picked = starts[:, :, None] + (nodes[None, :, None] - starts[:, :, None] + 1 + offsets) % spans[:, :, None]
    result = jnp.where(places[None, None, :] < degree[:, :, None], picked, -1)
    return result.reshape(GROUPS * NODE_DEV, DEG).astype(jnp.int32)


def with_spikes(entries, own_key, source, target, parts, factor):
    owner, partner = [(jnp.arange(entries.shape[position]) // (entries.shape[position] // parts)).reshape([-1 if axis == position else 1 for axis in range(entries.ndim)]) for position in (source, target)]
    chosen = jax.random.permutation(own_key, parts)[partner]
    strong = (owner == chosen) | (owner == (partner + parts // 2) % parts)
    return jnp.where(strong, factor * entries, entries)


def steps_of(own_key, dims, split, low, high):
    gain = 1.0
    for axis_at, shards_of in split:
        steps = jax.random.uniform(jax.random.fold_in(jax.random.fold_in(own_key, 6), axis_at), (shards_of,), jnp.float32, low / len(split), high / len(split))
        gain = gain * jnp.repeat(jnp.exp(steps), dims[axis_at] // shards_of).reshape((-1,) + (1,) * (len(dims) - 1 - axis_at))
    return gain


def centred(key, dims, scale, reach, cuts=(), kind=jnp.bfloat16):
    drawn = jax.random.normal(key, dims, jnp.float32) * scale
    if len(cuts) > 0:
        drawn = steps_of(key, dims, cuts, -0.22, 0.18) * drawn
    return jnp.clip(drawn, min=-reach, max=reach).astype(kind)


def bell_draw_with(rng, extent, scale, most, cuts, heavy, kind=jnp.bfloat16):
    array = scale * jax.random.normal(rng, extent, jnp.float32)
    if cuts:
        array = array * steps_of(rng, extent, cuts, -0.22, 0.18)
    return jnp.clip(with_spikes(array, jax.random.fold_in(rng, 3), *heavy), -most, most).astype(kind)


def setup_inputs(seed: int = 0) -> dict:
    streams_of = jax.random.split(jax.random.key(seed), 7)
    features = centred(streams_of[0], (NODES, HID), 1.0, 6.0, ((0, 8), (1, 4)))
    neighbour_lists = draw_neighbour_lists(jax.random.fold_in(streams_of[6], 71), 0)
    node_counts = draw_node_counts(jax.random.fold_in(streams_of[6], 71), 0)
    weight = centred(streams_of[3], (HID, HID), (HID // 8) ** -0.5, 0.375, ((1, 4),))
    bias_terms = centred(streams_of[4], (HID,), 0.3, 1.796875, ((0, 4),))
    cotangent = bell_draw_with(streams_of[5], (NODES, HID), 1.0, 6.0, ((0, 8), (1, 4)), (0, 1, 8, 2.0))
    return {"features": features, "neighbour_lists": neighbour_lists, "node_counts": node_counts, "weight": weight, "bias_terms": bias_terms, "cotangent": cotangent}


@jax.custom_vjp
def low(v):
    return lax.optimization_barrier(v.astype(jnp.bfloat16)).astype(jnp.float32)

@jax.custom_vjp
def low_back(v):
    return v

def low_keep(v):
    return (low(v), None)

def low_pass(kept, grad):
    return (grad,)

def back_keep(v):
    return (v, None)

def back_low(kept, grad):
    return (low(grad),)
low.defvjp(low_keep, low_pass)
low_back.defvjp(back_keep, back_low)

def aggregate(features, neighbour_lists):
    present = neighbour_lists >= 0
    clamped = jnp.where(present, neighbour_lists, jnp.zeros_like(neighbour_lists)).astype(jnp.int32)
    factors = jnp.where(present, jnp.float32(1.0), jnp.float32(0.0)).astype(jnp.float32)
    degree = lax.optimization_barrier(jnp.sum(factors, axis=1))
    summed = 2.0 * features
    for column in range(DEG):
        summed = summed + jnp.take(features, clamped[:, column], axis=0) * factors[:, column:column + 1]
    return summed / (degree + jnp.float32(1.0))[:, None]

def layer_group(inputs, weight, bias_terms):
    features, group_lists, count = inputs
    aggregated = low_back(low(aggregate(features, group_lists)))
    linear = low_back(jnp.dot(aggregated, weight, preferred_element_type=jnp.float32, precision=lax.Precision.HIGHEST) + bias_terms)
    slots = jnp.arange(NODE_DEV, dtype=jnp.int32)
    living = jnp.where(slots < count.astype(jnp.int32), jnp.float32(1.0), jnp.float32(0.0)).astype(jnp.float32)
    return jax.nn.silu(linear) * living[:, None]

def reference(features, neighbour_lists, node_counts, weight, bias_terms, cotangent):
    grouped = features.astype(jnp.float32).reshape(N_DP, NODE_DEV, HID)
    grouped_lists = neighbour_lists.astype(jnp.int32).reshape(N_DP, NODE_DEV, DEG)
    counts = node_counts.astype(jnp.int32)

    def forward(grouped_features, weight_float, bias_float):

        def one_group(inputs):
            return layer_group(inputs, weight_float, bias_float)
        return lax.map(jax.checkpoint(one_group), (grouped_features, grouped_lists, counts))
    result, pullback = jax.vjp(forward, grouped, weight.astype(jnp.float32), bias_terms.astype(jnp.float32))
    grads = pullback(cotangent.astype(jnp.float32).reshape(N_DP, NODE_DEV, HID))
    output = result.reshape(N_DP * NODE_DEV, HID).astype(jnp.bfloat16)
    features_grad = grads[0].reshape(N_DP * NODE_DEV, HID).astype(jnp.bfloat16)
    return (output, features_grad, grads[1], grads[2])
```

```python
import functools

import jax
import jax.numpy as jnp
from jax import lax
from jax.experimental import pallas as pl
from jax.experimental.pallas import tpu as pltpu
from jax.sharding import PartitionSpec as P

BF16 = jnp.bfloat16
F32 = jnp.float32
SLABS = 4
LANES = 128
VMEM_LIMIT = 48 << 20


def count_kernel(base, where_ref, packed_ref, lists_ref, feat_ref, counts_ref, same_ref, other_ref):
    rows, slots = lists_ref.shape
    step = pl.program_id(0)
    side = where_ref[0] % 2
    steps = pl.num_programs(0)
    block = (step + side * (steps // 2)) % steps
    row = lax.broadcasted_iota(jnp.int32, (LANES, 8 * slots), 0)
    owner = lax.broadcasted_iota(jnp.int32, (1, 8 * slots), 1) // slots

    def group(index):
        entry = packed_ref[index : index + 1, :]
        high = (entry >> 7) * 8 + owner
        low = entry & (LANES - 1)
        left = jnp.where(high == row, 1.0, 0.0).astype(BF16)
        right = jnp.where(low == row, 1.0, 0.0).astype(BF16)
        return lax.dot_general(left, right, (((1,), (1,)), ((), ())), preferred_element_type=F32)

    for pair in range(rows // 16):
        first, second = group(2 * pair), group(2 * pair + 1)
        for tile in range(counts_ref.shape[1] // LANES):
            counts_ref[pair * 16 : (pair + 1) * 16, tile * LANES : (tile + 1) * LANES] = jnp.concatenate(
                [first[tile * 8 : (tile + 1) * 8], second[tile * 8 : (tile + 1) * 8]], 0
            ).astype(BF16)
    down = lax.broadcasted_iota(jnp.int32, (LANES, LANES), 0)
    across = lax.broadcasted_iota(jnp.int32, (LANES, LANES), 1)
    twice = jnp.where(down == across, 2.0, 0.0)
    column = pl.multiple_of(base + block * rows, LANES)
    tile_view = counts_ref[:, pl.ds(column, LANES)].astype(F32)
    counts_ref[:, pl.ds(column, LANES)] = (tile_view + twice).astype(BF16)
    degree = jnp.sum(jnp.where(lists_ref[...] >= 0, 1.0, 0.0), axis=1, keepdims=True)
    total = jnp.dot(counts_ref[...], feat_ref[...], preferred_element_type=F32)
    result = (total / (degree + 1.0)).astype(BF16)

    @pl.when(step < steps // 2)
    def _():
        same_ref[...] = result

    @pl.when(step >= steps // 2)
    def _():
        other_ref[...] = result


def count_call(where, packed, lists, features, base, size):
    nodes, slots = lists.shape
    width = features.shape[1]
    rows = LANES
    steps = size // rows
    half = steps // 2

    def natural(step, where_ref):
        return (step + (where_ref[0] % 2) * half) % steps

    return pl.pallas_call(
        functools.partial(count_kernel, base),
        grid_spec=pltpu.PrefetchScalarGridSpec(
            num_scalar_prefetch=1,
            grid=(steps,),
            in_specs=[
                pl.BlockSpec((rows // 8, 8 * slots), lambda i, w: (base // rows + natural(i, w), 0)),
                pl.BlockSpec((rows, slots), lambda i, w: (base // rows + natural(i, w), 0)),
                pl.BlockSpec((nodes, width), lambda i, w: (0, 0)),
            ],
            out_specs=[
                pl.BlockSpec((rows, nodes), lambda i, w: (natural(i, w), 0)),
                pl.BlockSpec((rows, width), lambda i, w: (jnp.minimum(i, half - 1), 0)),
                pl.BlockSpec((rows, width), lambda i, w: (jnp.maximum(i - half, 0), 0)),
            ],
        ),
        out_shape=[
            jax.ShapeDtypeStruct((size, nodes), BF16),
            jax.ShapeDtypeStruct((size // 2, width), BF16),
            jax.ShapeDtypeStruct((size // 2, width), BF16),
        ],
        compiler_params=pltpu.CompilerParams(vmem_limit_bytes=VMEM_LIMIT),
        cost_estimate=pl.CostEstimate(
            flops=2 * size * nodes * (width + 512), bytes_accessed=2 * nodes * (size + width), transcendentals=0
        ),
        name="count_and_aggregate",
    )(where, packed, lists, features)


def row_kernel(
    base, where_ref, live_ref, part0, part1, part2, part3, cot_own, cot_sib, weight_own, weight_sib, bias_own, bias_sib,
    out_own, out_sib, grad_own, grad_sib, back0, back1, back2, back3,
):
    rows, width = cot_sib.shape
    place = where_ref[0]
    first = base + (place % 2) * rows
    slot = first + lax.broadcasted_iota(jnp.int32, (rows, width), 0)
    living = slot < live_ref[0]
    parts = (part0, part1, part2, part3)
    starts = [pl.multiple_of((place ^ code) * width, LANES) for code in range(4)]
    grads = []
    for weight, bias, cot, out, grad in (
        (weight_own, bias_own, cot_own, out_own, grad_own),
        (weight_sib, bias_sib, cot_sib, out_sib, grad_sib),
    ):
        linear = bias[...].astype(F32)
        for part, start in zip(parts, starts):
            linear = linear + jnp.dot(part[...], weight[pl.ds(start, width), :], preferred_element_type=F32)
        sigma = 1.0 / (1.0 + jnp.exp(-linear))
        out[...] = jnp.where(living, linear * sigma, 0.0).astype(BF16)
        slope = sigma * (1.0 + linear * (1.0 - sigma))
        value = jnp.where(living, cot[...].astype(F32) * slope, 0.0).astype(BF16)
        grad[...] = value
        grads.append(value)
    for back, start in zip((back0, back1, back2, back3), starts):
        total = jnp.zeros((rows, width), F32)
        for weight, value in zip((weight_own, weight_sib), grads):
            total = total + lax.dot_general(
                value, weight[pl.ds(start, width), :], (((1,), (1,)), ((), ())), preferred_element_type=F32
            )
        back[...] = total.astype(BF16)


def row_call(where, live, parts, cotangent, cot_sib, weight_own, weight_sib, bias_own, bias_sib, base):
    rows, width = cot_sib.shape
    depth = weight_own.shape[0]
    whole = lambda shape: pl.BlockSpec(shape, lambda i, w, c: (0, 0))
    chunk = whole((rows, width))
    return pl.pallas_call(
        functools.partial(row_kernel, base),
        grid_spec=pltpu.PrefetchScalarGridSpec(
            num_scalar_prefetch=2,
            grid=(1,),
            in_specs=[chunk] * 4
            + [pl.BlockSpec((rows, width), lambda i, w, c: (base // rows + w[0] % 2, 0)), chunk]
            + [whole((depth, width))] * 2
            + [whole((1, width))] * 2,
            out_specs=[chunk] * 8,
        ),
        out_shape=[jax.ShapeDtypeStruct((rows, width), BF16)] * 8,
        compiler_params=pltpu.CompilerParams(vmem_limit_bytes=VMEM_LIMIT),
        cost_estimate=pl.CostEstimate(
            flops=2 * 2 * rows * depth * 2 * width, bytes_accessed=2 * (14 * rows + 2 * depth) * width, transcendentals=rows * width * 2
        ),
        name="linear_and_slope",
    )(where, live, *parts, cotangent, cot_sib, weight_own, weight_sib, bias_own, bias_sib)


def product_kernel(slabs, where_ref, *refs):
    parts, grads, (kept, given) = refs[: 4 * slabs], refs[4 * slabs : 6 * slabs], refs[6 * slabs :]
    width = parts[0].shape[1]
    for half in range(2):
        for code in range(4):
            total = jnp.zeros((width, width), F32)
            for slab in range(slabs):
                total = total + lax.dot_general(
                    parts[4 * slab + code][...],
                    grads[2 * slab + half][...],
                    (((0,), (0,)), ((), ())),
                    preferred_element_type=F32,
                )
            block = where_ref[0] ^ code
            rows = pl.ds(pl.multiple_of((block % 2) * width, LANES), width)
            result = total.astype(BF16)

            @pl.when(block // 2 == where_ref[1])
            def _(half=half, rows=rows, result=result):
                kept[half, rows, :] = result

            @pl.when(block // 2 != where_ref[1])
            def _(half=half, rows=rows, result=result):
                given[half, rows, :] = result


def product_call(where, parts, grads):
    slabs = len(parts)
    rows, width = parts[0][0].shape
    operands = [p for quad in parts for p in quad] + [g for pair in grads for g in pair]
    outs = (2, 2 * width, width)
    return pl.pallas_call(
        functools.partial(product_kernel, slabs),
        grid_spec=pltpu.PrefetchScalarGridSpec(
            num_scalar_prefetch=1,
            grid=(1,),
            in_specs=[pl.BlockSpec((rows, width), lambda i, w: (0, 0))] * len(operands),
            out_specs=[pl.BlockSpec(outs, lambda i, w: (0, 0, 0))] * 2,
        ),
        out_shape=[jax.ShapeDtypeStruct(outs, BF16)] * 2,
        compiler_params=pltpu.CompilerParams(vmem_limit_bytes=VMEM_LIMIT),
        name="weight_product",
    )(where, *operands)


def spread_kernel(slabs, final, where_ref, *refs):
    side = where_ref[0] % 2
    out, scaled = refs[-2], refs[-1]
    total = refs[-3][...] if final else None
    for slab in range(slabs):
        counts, lists, near, level, far, cross = refs[6 * slab : 6 * slab + 6]
        rows = near.shape[0]
        mine = pl.multiple_of(side * rows, LANES)
        theirs = pl.multiple_of((1 - side) * rows, LANES)
        scaled[pl.ds(mine, rows), :] = near[...].astype(F32) + far[...].astype(F32)
        scaled[pl.ds(theirs, rows), :] = level[...].astype(F32) + cross[...].astype(F32)
        degree = jnp.sum(jnp.where(lists[...] >= 0, 1.0, 0.0), axis=1, keepdims=True)
        value = (scaled[...] / (degree + 1.0)).astype(BF16)
        term = lax.dot_general(counts[...], value, (((0,), (0,)), ((), ())), preferred_element_type=F32)
        total = term if total is None else total + term
    out[...] = total.astype(out.dtype)


def spread_call(where, lists, entries, slab_at, partial):
    slabs = len(entries)
    size, nodes = entries[0][0].shape
    rows, width = entries[0][1].shape
    slots = lists.shape[1]
    tile = 512
    operands, specs = [], []
    for index, entry in enumerate(entries):
        counts, backs = entry[0], entry[1:]
        at = slab_at[index]
        operands += [counts, lists, *backs]
        specs += [
            pl.BlockSpec((size, tile), lambda i, w: (0, i)),
            pl.BlockSpec((size, slots), lambda i, w, at=at: (at, 0)),
        ] + [pl.BlockSpec((rows, width), lambda i, w: (0, 0))] * 4
    final = partial is not None
    if final:
        operands.append(partial)
        specs.append(pl.BlockSpec((tile, width), lambda i, w: (i, 0)))
    return pl.pallas_call(
        functools.partial(spread_kernel, slabs, final),
        grid_spec=pltpu.PrefetchScalarGridSpec(
            num_scalar_prefetch=1,
            grid=(nodes // tile,),
            in_specs=specs,
            out_specs=pl.BlockSpec((tile, width), lambda i, w: (i, 0)),
            scratch_shapes=[pltpu.VMEM((size, width), F32)],
        ),
        out_shape=jax.ShapeDtypeStruct((nodes, width), BF16 if final else F32),
        compiler_params=pltpu.CompilerParams(vmem_limit_bytes=VMEM_LIMIT),
        name="spread_back",
    )(where, *operands)


def local(features, neighbour_lists, node_counts, weight, bias_terms, cotangent):
    dp_count = lax.axis_size("dp")
    mp_count = lax.axis_size("mp")
    bits = dp_count.bit_length() - 1
    place = lax.axis_index("mp")
    line = lax.axis_index("dp")
    side = place % 2
    core = line % 2
    where = place.astype(jnp.int32).reshape(1)
    nodes, width = features.shape
    depth = weight.shape[0]
    slots = neighbour_lists.shape[1]
    size = nodes // SLABS
    rows = size // 2
    live = node_counts.astype(jnp.int32)

    def across(value, code):
        return lax.ppermute(value, "mp", [(i, i ^ code) for i in range(mp_count)])

    orders = (list(range(1, bits)), list(range(bits - 1, 0, -1)))

    def along(value, stage):
        return lax.ppermute(value, "dp", [(i, i ^ (1 << orders[i % 2][stage])) for i in range(dp_count)])

    def over_core(value):
        return lax.ppermute(value, "dp", [(i, i ^ 1) for i in range(dp_count)])

    def stage_bit(stage):
        return jnp.where(core == 0, (line >> orders[0][stage]) & 1, (line >> orders[1][stage]) & 1)

    def join(mine, theirs, bit, axis=0):
        return jnp.where(
            bit == 0, jnp.concatenate([mine, theirs], axis), jnp.concatenate([theirs, mine], axis)
        )

    def gather_pieces(piece):
        for stage in range(bits - 1):
            piece = join(piece, along(piece, stage), stage_bit(stage))
        return join(piece, over_core(piece), core)

    piece_rows = depth // dp_count
    offset = core * (depth // 2)
    for stage in range(bits - 1):
        offset = offset + stage_bit(stage) * (piece_rows << stage)

    bias_own = bias_terms.reshape(1, width)
    bias_sib = across(bias_own, 1)
    weight_sib = gather_pieces(across(lax.dynamic_slice_in_dim(weight, offset, piece_rows, 0), 1))

    packed = neighbour_lists.reshape(nodes // 8, 8 * slots)
    cot_send = lax.dynamic_index_in_dim(cotangent.reshape(SLABS, 2, rows, width), 1 - side, 1, False)
    cot_sibs = [across(cot_send[slab], 1) for slab in range(SLABS)]
    counts, parts = [], []
    for slab in range(SLABS):
        block, same, other = count_call(where, packed, neighbour_lists, features, slab * size, size)
        counts.append(block)
        parts.append((same, across(other, 1), across(same, 2), across(other, 3)))
    out_pairs, grads, entries = [], [], []
    for slab in range(SLABS):
        results = row_call(
            where, live, parts[slab], cotangent, cot_sibs[slab], weight, weight_sib, bias_own, bias_sib, slab * size
        )
        out_own, out_sib, grad_own, grad_sib = results[:4]
        backs = results[4:]
        out_pairs.append((out_own, across(out_sib, 1)))
        grads.append((grad_own, grad_sib))
        entries.append((counts[slab], backs[0], across(backs[1], 1), across(backs[2], 2), across(backs[3], 3)))

    kept, given = product_call(jnp.stack([place, core]).astype(jnp.int32), parts, grads)
    terms = (kept.astype(F32) + over_core(given).astype(F32)).astype(BF16)

    def halve(value, bit, send):
        length = value.shape[1] // 2
        kept = lax.dynamic_slice_in_dim(value, bit * length, length, 1)
        given = lax.dynamic_slice_in_dim(value, (1 - bit) * length, length, 1)
        return (kept.astype(F32) + send(given).astype(F32)).astype(BF16)

    for stage in range(bits - 2, -1, -1):
        terms = halve(terms, stage_bit(stage), lambda v, stage=stage: along(v, stage))
    share = terms[0].astype(F32) + across(terms[1], 1).astype(F32)
    weight_grad = gather_pieces(share.astype(BF16)).astype(F32)

    sums = jnp.stack(
        [sum(jnp.sum(g[half].astype(F32), axis=0) for g in grads) for half in range(2)]
    )
    sums = sums + over_core(sums)
    for stage in range(bits - 1):
        sums = sums + along(sums, stage)
    bias_grad = sums[0] + across(sums[1], 1)

    output = jnp.concatenate([join(mine, theirs, side) for mine, theirs in out_pairs], 0)
    partial = spread_call(where, neighbour_lists, entries[:-1], list(range(SLABS - 1)), None)
    features_grad = spread_call(where, neighbour_lists, entries[-1:], [SLABS - 1], partial)
    return (output, features_grad, weight_grad, bias_grad)


def solution(mesh):
    in_specs = (P("dp", "mp"), P("dp", None), P("dp"), P(None, "mp"), P("mp"), P("dp", "mp"))
    out_specs = (P("dp", "mp"), P("dp", "mp"), P(None, "mp"), P("mp"))
    return jax.shard_map(local, mesh=mesh, in_specs=in_specs, out_specs=out_specs, check_vma=False)
```

```python
import functools

import jax
import jax.numpy as jnp
from jax import lax
from jax.experimental import pallas as pl
from jax.experimental.pallas import tpu as pltpu
from jax.sharding import PartitionSpec as P

BF16 = jnp.bfloat16
F32 = jnp.float32
GROUPS = ((4,), (4,))
LANES = 128
PAD = 16
VMEM_LIMIT = 48 << 20
SMALL = pl.CostEstimate(flops=1, bytes_accessed=1, transcendentals=0)
ANY = pl.BlockSpec(memory_space=pl.ANY)


def like(*shape, dtype=BF16):
    return jax.ShapeDtypeStruct(shape, dtype)


def fixed(*shape):
    return pl.BlockSpec(shape, lambda *_: (0,) * len(shape))


def call(kernel, name, scalars, operands, out_shape, in_specs=None, out_specs=None, grid=(1,), scratch=(), aliases=None):
    if in_specs is None:
        in_specs = [fixed(*o.shape) for o in operands]
    if out_specs is None:
        out_specs = [fixed(*o.shape) for o in out_shape]
    return pl.pallas_call(
        kernel,
        grid_spec=pltpu.PrefetchScalarGridSpec(
            num_scalar_prefetch=len(scalars), grid=grid, in_specs=in_specs, out_specs=out_specs, scratch_shapes=scratch
        ),
        out_shape=out_shape,
        compiler_params=pltpu.CompilerParams(vmem_limit_bytes=VMEM_LIMIT),
        input_output_aliases={len(scalars) + i: o for i, o in (aliases or {}).items()},
        cost_estimate=SMALL,
        name=name,
    )(*scalars, *operands)


def piece_kernel(at, weight, bias, out):
    rows = out.shape[0] - PAD
    out[:rows, :] = weight[...]
    out[rows:, :] = jnp.broadcast_to(bias[...].astype(F32), (PAD, out.shape[1])).astype(BF16)


def piece_call(at, weight, bias, rows):
    width = weight.shape[1]
    return call(
        piece_kernel,
        "weight_piece",
        (at,),
        (weight, bias),
        [like(rows + PAD, width)],
        in_specs=[pl.BlockSpec((rows, width), lambda i, s: (s[3], 0)), fixed(1, width)],
    )[0]


def count_kernel(base, slots, at, packed_ref, feat_ref, cot_ref, *refs):
    counts_ref, same_ref, other_ref, pack_ref, scale_ref = refs[-5:]
    rows = counts_ref.shape[0]
    step = pl.program_id(0)
    steps = pl.num_programs(0)
    block = (step + at[1] * (steps // 2)) % steps
    row = lax.broadcasted_iota(jnp.int32, (LANES, 8 * slots), 0)
    owner = lax.broadcasted_iota(jnp.int32, (1, 8 * slots), 1) // slots

    def group(index):
        entry = packed_ref[index : index + 1, :]
        high = (entry >> 7) * 8 + owner
        low = entry & (LANES - 1)
        left = jnp.where(high == row, 1.0, 0.0).astype(BF16)
        right = jnp.where(low == row, 1.0, 0.0).astype(BF16)
        return lax.dot_general(left, right, (((1,), (1,)), ((), ())), preferred_element_type=F32)

    for pair in range(rows // 16):
        first, second = group(2 * pair), group(2 * pair + 1)
        for tile in range(counts_ref.shape[1] // LANES):
            counts_ref[pair * 16 : (pair + 1) * 16, tile * LANES : (tile + 1) * LANES] = jnp.concatenate(
                [first[tile * 8 : (tile + 1) * 8], second[tile * 8 : (tile + 1) * 8]], 0
            ).astype(BF16)
    degree = jnp.sum(counts_ref[...].astype(F32), axis=1, keepdims=True)
    scale = 1.0 / (degree + 1.0)
    down = lax.broadcasted_iota(jnp.int32, (LANES, LANES), 0)
    across = lax.broadcasted_iota(jnp.int32, (LANES, LANES), 1)
    twice = jnp.where(down == across, 2.0, 0.0)
    column = pl.multiple_of(base + block * rows, LANES)
    tile_view = counts_ref[:, pl.ds(column, LANES)].astype(F32)
    counts_ref[:, pl.ds(column, LANES)] = (tile_view + twice).astype(BF16)
    total = jnp.dot(counts_ref[...], feat_ref[...], preferred_element_type=F32)
    result = (total * scale).astype(BF16)

    @pl.when(step < steps // 2)
    def _():
        same_ref[...] = result
        scale_ref[...] = scale

    @pl.when(step >= steps // 2)
    def _():
        other_ref[...] = result
        pack_ref[0] = result
        pack_ref[1] = cot_ref[...]


def count_call(at, packed, features, cotangent, base, size, counts):
    nodes, width = features.shape
    slots = packed.shape[1] // 8
    rows = LANES
    steps = size // rows
    half = steps // 2

    def natural(i, s):
        return base // rows + (i + s[1] * half) % steps

    def early(i, s):
        return jnp.minimum(i, half - 1), 0

    def late(i, s):
        return jnp.maximum(i - half, 0), 0

    operands = [packed, features, cotangent]
    specs = [
        pl.BlockSpec((rows // 8, 8 * slots), lambda i, s: (natural(i, s), 0)),
        fixed(nodes, width),
        pl.BlockSpec((rows, width), lambda i, s: (natural(i, s), 0)),
    ]
    aliases = {}
    if counts is not None:
        aliases = {len(operands): 0}
        operands.append(counts)
        specs.append(ANY)
    return call(
        functools.partial(count_kernel, base, slots),
        "count_and_aggregate",
        (at,),
        operands,
        [
            like(nodes, nodes),
            like(size // 2, width),
            like(size // 2, width),
            like(2, size // 2, width),
            like(size // 2, 1, dtype=F32),
        ],
        in_specs=specs,
        out_specs=[
            pl.BlockSpec((rows, nodes), lambda i, s: (natural(i, s), 0)),
            pl.BlockSpec((rows, width), early),
            pl.BlockSpec((rows, width), late),
            pl.BlockSpec((2, rows, width), lambda i, s: (0, *late(i, s))),
            pl.BlockSpec((rows, 1), early),
        ],
        grid=(steps,),
        aliases=aliases,
    )


def row_kernel(
    base, at, live, part0, near, part2, part3, scale, cot_own, weight_own, weight_sib, bias_own, bias_sib, *refs
):
    out_own, grads, back0, back_near, back2, back3 = refs[-6:]
    rows, width = part0.shape
    place = at[0]
    slot = base + at[1] * rows + lax.broadcasted_iota(jnp.int32, (rows, width), 0)
    living = slot < live[0]
    starts = [pl.multiple_of((place ^ code) * width, LANES) for code in range(4)]
    values = []
    for half, (weight, bias, cot) in enumerate(
        ((weight_own, bias_own, cot_own[...]), (weight_sib, bias_sib, near[1]))
    ):
        linear = bias[...].astype(F32)
        for part, start in zip((part0[...], near[0], part2[...], part3[...]), starts):
            linear = linear + jnp.dot(part, weight[pl.ds(start, width), :], preferred_element_type=F32)
        sigma = 1.0 / (1.0 + jnp.exp(-linear))
        result = jnp.where(living, linear * sigma, 0.0).astype(BF16)
        if half == 0:
            out_own[...] = result
        else:
            back_near[0] = result
        slope = sigma * (1.0 + linear * (1.0 - sigma))
        value = jnp.where(living, cot.astype(F32) * slope, 0.0).astype(BF16)
        grads[at[1] if half == 0 else 1 - at[1]] = value
        values.append(value)
    for code, start in enumerate(starts):
        total = jnp.zeros((rows, width), F32)
        for weight, value in zip((weight_own, weight_sib), values):
            total = total + lax.dot_general(
                value, weight[pl.ds(start, width), :], (((1,), (1,)), ((), ())), preferred_element_type=F32
            )
        total = (total * scale[...]).astype(BF16)
        if code == 1:
            back_near[1] = total
        else:
            (back0, None, back2, back3)[code][...] = total


def row_call(at, live, parts, scale, cotangent, weight_own, weight_sib, bias_own, bias_sib, base, start, all_rows, buffers):
    rows, width = parts[0].shape
    operands = [*parts, scale, cotangent, weight_own, weight_sib, bias_own, bias_sib]
    specs = [fixed(*o.shape) for o in operands]
    specs[5] = pl.BlockSpec((rows, width), lambda i, s, c: (base // rows + s[1], 0))
    flat, pair = like(all_rows, width), like(2, all_rows, width)
    here = (base - start) // 2 // rows
    flat_spec = pl.BlockSpec((rows, width), lambda i, s, c: (here, 0))
    pair_spec = pl.BlockSpec((2, rows, width), lambda i, s, c: (0, here, 0))
    aliases = {}
    if buffers is not None:
        aliases = {len(operands) + i: i for i in range(len(buffers))}
        operands += buffers
        specs += [ANY] * len(buffers)
    return call(
        functools.partial(row_kernel, base),
        "linear_and_slope",
        (at, live),
        operands,
        [flat, pair, flat, pair, flat, flat],
        in_specs=specs,
        out_specs=[flat_spec, pair_spec, flat_spec, pair_spec, flat_spec, flat_spec],
        aliases=aliases,
    )


def put_sums(ref, index, value):
    high = value.astype(BF16)
    low = (value - high.astype(F32)).astype(BF16)
    row = lax.broadcasted_iota(jnp.int32, (PAD, value.shape[1]), 0)
    both = jnp.where(row == 0, high.astype(F32), jnp.where(row == 1, low.astype(F32), 0.0))
    ref[(*index, slice(ref.shape[-2] - PAD, None), slice(None))] = both.astype(BF16)


def get_sums(ref, index):
    rows = ref[(*index, slice(ref.shape[-2] - PAD, None), slice(None))]
    return jnp.sum(rows.astype(F32), axis=0, keepdims=True)


def product_kernel(at, *refs):
    groups, refs, terms = len(GROUPS), refs[:-1], refs[-1]
    parts, grads = refs[:-groups], refs[-groups:]
    slabs = len(parts) // 4
    slices = []
    for group, units in enumerate(GROUPS):
        low = 0
        for _ in units:
            high = low + parts[4 * len(slices)].shape[-2]
            slices.append((group, slice(low, high)))
            low = high
    width = parts[0].shape[-1]
    for half in range(2):
        for code in range(4):
            total = jnp.zeros((width, width), F32)
            for slab in range(slabs):
                part = parts[4 * slab + code]
                part = part[0] if code == 1 else part[...]
                total = total + lax.dot_general(
                    part,
                    grads[slices[slab][0]][half, slices[slab][1], :],
                    (((0,), (0,)), ((), ())),
                    preferred_element_type=F32,
                )
            block = at[0] ^ code
            rows = pl.ds(pl.multiple_of((block % 2) * width, LANES), width)
            terms[block // 2, half, rows, :] = total.astype(BF16)
        sums = sum(jnp.sum(grad[half].astype(F32), axis=0, keepdims=True) for grad in grads)
        for side in range(2):
            put_sums(terms, (side, half), sums)


def product_call(at, parts, grads):
    width = grads[0].shape[-1]
    operands = [p for quad in parts for p in quad] + list(grads)
    return call(product_kernel, "weight_product", (at,), operands, [like(2, 2, 2 * width + PAD, width)])[0]


def fold_kernel(at, came, out):
    rows = out.shape[2] - PAD
    for half in range(2):
        sums = get_sums(came, (0, half)) + get_sums(came, (1, half))
        for part in range(2):
            low, high = part * rows, (part + 1) * rows
            total = came[0, half, low:high, :].astype(F32) + came[1, half, low:high, :].astype(F32)
            out[part, half, :rows, :] = total.astype(BF16)
            put_sums(out, (part, half), sums)


def fold_call(at, came):
    length, width = came.shape[2:]
    return call(fold_kernel, "fold_terms", (at,), (came,), [like(2, 2, (length - PAD) // 2 + PAD, width)])[0]


def part_kernel(at, came, out):
    rows = out.shape[1] - PAD
    for half in range(2):
        out[half, :rows, :] = (came[0, half, :rows, :].astype(F32) + came[1, half, :rows, :].astype(F32)).astype(BF16)
        put_sums(out, (half,), get_sums(came, (0, half)) + get_sums(came, (1, half)))


def part_call(at, came):
    return call(part_kernel, "part_terms", (at,), (came,), [like(*came.shape[1:])])[0]


def share_kernel(at, came, share, sums):
    rows = share.shape[1]
    total = (came[0, :rows, :].astype(F32) + came[1, :rows, :].astype(F32)).astype(BF16)
    share[0] = total
    share[1] = total
    sums[...] = get_sums(came, (0,)) + get_sums(came, (1,))


def share_call(at, came):
    two, length, width = came.shape
    return call(
        share_kernel, "share_terms", (at,), (came,), [like(2, length - PAD, width), like(1, width, dtype=F32)]
    )


def place_kernel(groups, at, *refs):
    out = refs[-1]
    for bases, mine, theirs in zip(groups, refs[0:-1:2], refs[1:-1:2]):
        for low, high in zip(bases, bases[1:]):
            rows = (high - low) // 2
            part = slice((low - bases[0]) // 2, (high - bases[0]) // 2)
            out[pl.ds(pl.multiple_of(low + at[1] * rows, 16), rows), :] = mine[part, :]
            out[pl.ds(pl.multiple_of(low + (1 - at[1]) * rows, 16), rows), :] = theirs[0, part, :]


def place_call(at, groups, pairs):
    width = pairs[0][0].shape[1]
    operands = [o for pair in pairs for o in pair]
    specs = [s for mine, _ in pairs for s in (fixed(*mine.shape), fixed(1, *mine.shape))]
    return call(
        functools.partial(place_kernel, groups), "place_rows", (at,), operands, [like(groups[-1][-1], width)], in_specs=specs
    )[0]


def spread_kernel(bases, final, at, counts, level, near, far, cross, *refs):
    out, scaled = refs[-2:]

    @pl.when(pl.program_id(0) == 0)
    def _():
        for low, high in zip(bases, bases[1:]):
            rows = (high - low) // 2
            low = low - bases[0]
            part = slice(low // 2, low // 2 + rows)
            mine = pl.ds(pl.multiple_of(low + at[1] * rows, LANES), rows)
            theirs = pl.ds(pl.multiple_of(low + (1 - at[1]) * rows, LANES), rows)
            scaled[mine, :] = (level[part, :].astype(F32) + far[part, :].astype(F32)).astype(BF16)
            scaled[theirs, :] = (near[0, part, :].astype(F32) + cross[part, :].astype(F32)).astype(BF16)

    total = lax.dot_general(counts[...], scaled[...], (((0,), (0,)), ((), ())), preferred_element_type=F32)
    if final:
        total = total + refs[0][...]
    out[...] = total.astype(out.dtype)


def spread_call(at, bases, counts, level, near, far, cross, partial, final):
    nodes = counts.shape[1]
    rows, width = level.shape
    tile = 512
    here = bases[0] // (2 * rows)
    operands = [counts, level, near, far, cross]
    specs = [
        pl.BlockSpec((2 * rows, tile), lambda i, s: (here, i)),
        fixed(rows, width),
        pl.BlockSpec((1, rows, width), lambda i, s: (1, 0, 0)),
        fixed(rows, width),
        fixed(rows, width),
    ]
    tiled = pl.BlockSpec((tile, width), lambda i, s: (i, 0))
    if partial is not None:
        operands.append(partial)
        specs.append(tiled)
    return call(
        functools.partial(spread_kernel, bases, partial is not None),
        "spread_back",
        (at,),
        operands,
        [like(nodes, width, dtype=BF16 if final else F32)],
        in_specs=specs,
        out_specs=[tiled],
        grid=(nodes // tile,),
        scratch=[pltpu.VMEM((2 * rows, width), BF16)],
    )[0]


def tie(value, *after):
    return lax.optimization_barrier((value, *after))[0]


def local(features, neighbour_lists, node_counts, weight, bias_terms, cotangent):
    dp_count = lax.axis_size("dp")
    mp_count = lax.axis_size("mp")
    bits = dp_count.bit_length() - 1
    place = lax.axis_index("mp")
    line = lax.axis_index("dp")
    core = line % 2
    nodes, width = features.shape
    depth = weight.shape[0]
    slots = neighbour_lists.shape[1]
    live = node_counts.astype(jnp.int32)
    orders = [(low, high) for low, high in zip(range(1, bits), range(bits - 1, 0, -1))] + [(0, 0)]
    piece_rows = depth // dp_count
    piece = jnp.int32(0)
    for stage, (low, high) in enumerate(orders):
        piece = piece + (jnp.where(core == 0, line >> low, line >> high) % 2 << stage)
    at = jnp.stack([place, place % 2, core, piece]).astype(jnp.int32)

    def across(value, code):
        return lax.ppermute(value, "mp", [(i, i ^ code) for i in range(mp_count)])

    def swap(value, stage):
        pairs = []
        for i in range(dp_count):
            bit = 1 << orders[stage][i % 2]
            if not i & bit:
                pairs.append([i, i | bit])
        return lax.all_to_all(value, "dp", 0, 0, axis_index_groups=pairs)

    def swap_sides(value):
        return lax.all_to_all(
            value, "mp", 0, 0, axis_index_groups=[[i, i + 1] for i in range(0, mp_count, 2)]
        )

    def gather_pieces(value):
        for stage in range(bits):
            value = swap(value, stage)
            value = value.reshape(-1, width)
            if stage < bits - 1:
                value = jnp.stack([value, value])
        return value

    unit = nodes // sum(map(sum, GROUPS))
    groups, low = [], 0
    for units in GROUPS:
        bases = [low]
        for length in units:
            low += length * unit
            bases.append(low)
        groups.append(bases)
    packed = neighbour_lists.reshape(nodes // 8, 8 * slots)
    counts, parts, scales = None, [], []
    bias_own = bias_terms.reshape(1, width)
    piece = across(piece_call(at, weight, bias_own, piece_rows), 1)
    slabs = [slab for bases in groups for slab in zip(bases, bases[1:])]

    def count_slab(slab, counts):
        low, high = slab
        return count_call(at, packed, features, cotangent, low, high - low, counts)

    def first_rows(piece, counts):
        rest = []
        for slab in slabs[1:]:
            rest.append(count_slab(slab, counts))
            counts = rest[-1][0]
        return gather_pieces(jnp.stack([piece[:piece_rows]] * 2)), [r[1:] for r in rest], counts

    def no_rows(piece, counts):
        return jax.tree.map(
            lambda shape: jnp.zeros(shape.shape, shape.dtype), jax.eval_shape(first_rows, piece, counts)
        )

    counts, *first = count_slab(slabs[0], None)
    first[:3] = [tie(value, piece) for value in first[:3]]
    weight_sib, rest, counts = lax.cond(live[0] > 0, first_rows, no_rows, piece, counts)
    bias_sib = piece[piece_rows : piece_rows + 1]
    for same, other, pack, scale in (first, *rest):
        parts.append((same, across(pack, 1), across(same, 2), across(other, 3)))
        scales.append(scale)

    sides, index = [], 0
    for bases in groups:
        buffers = None
        for low, high in zip(bases, bases[1:]):
            buffers = row_call(
                tie(at, scales[-1]), live, parts[index], scales[index], cotangent, weight, weight_sib, bias_own, bias_sib, low, bases[0],
                (bases[-1] - bases[0]) // 2, buffers,
            )
            index += 1
        sides.append(buffers)
    grads = [side[1] for side in sides]

    def fold_terms(parts, grads):
        came = swap(product_call(at, parts, grads), bits - 1)
        for stage in range(bits - 2, -1, -1):
            came = swap(fold_call(at, came), stage)
        return part_call(at, came)

    def no_terms(parts, grads):
        return jnp.zeros((2, piece_rows + PAD, width), BF16)

    def share_terms(came, counts, entry):
        share, bias_grad = share_call(at, came)
        partial = spread_call(at, groups[0], counts, *entry, None, False)
        return gather_pieces(share).astype(F32), bias_grad, partial

    def no_share(came, counts, entry):
        return jnp.zeros((depth, width), F32), jnp.zeros((1, width), F32), jnp.zeros((nodes, width), F32)

    terms = lax.cond(live[0] > 0, fold_terms, no_terms, parts, grads)
    pairs, entries = [], []
    for index, side in enumerate(sides):
        out_own, _, level, near, far, cross = side
        if index == 0:
            near, far, cross = (tie(value, parts[-1][2]) for value in (near, far, cross))
        if index == len(groups) - 1:
            came = swap_sides(tie(terms, *entries[0][1:]))
            near, far, cross = tie(near, came), tie(far, came), tie(cross, came)
        near, far, cross = across(near, 1), across(far, 2), across(cross, 3)
        pairs.append((out_own, near))
        entries.append((level, near, far, cross))
    weight_grad, bias_grad, partial = lax.cond(live[0] > 0, share_terms, no_share, came, counts, entries[0])
    features_grad = spread_call(at, groups[1], counts, *entries[1], partial, True)
    output = place_call(at, groups, pairs)
    return (output, features_grad, weight_grad, bias_grad.reshape(width))


def solution(mesh):
    in_specs = (P("dp", "mp"), P("dp", None), P("dp"), P(None, "mp"), P("mp"), P("dp", "mp"))
    out_specs = (P("dp", "mp"), P("dp", "mp"), P(None, "mp"), P("mp"))
    return jax.shard_map(local, mesh=mesh, in_specs=in_specs, out_specs=out_specs, check_vma=False)
```

```python
import functools

import jax
import jax.numpy as jnp
from jax import lax
from jax.experimental import pallas as pl
from jax.experimental.pallas import tpu as pltpu
from jax.sharding import PartitionSpec as P

BF16 = jnp.bfloat16
F32 = jnp.float32
UNITS = 8
SLABS = ((0, 4), (4, 4))
GROUPS = ((((0, 0), (0, 1)), ((1, 0),)), (((1, 1),),))
PARTS = tuple(tuple(entry for run in group for entry in run) for group in GROUPS)
LANES = 128
PAD = 16
VMEM_LIMIT = 48 << 20
ANY = pl.BlockSpec(memory_space=pl.ANY)


def like(*shape, dtype=BF16):
    return jax.ShapeDtypeStruct(shape, dtype)


def fixed(*shape):
    return pl.BlockSpec(shape, lambda *_: (0,) * len(shape))


def units_of(entry):
    slab, block = entry
    first, length = SLABS[slab]
    return first + block, first + length // 2 + block


def call(
    kernel, name, scalars, operands, out_shape, in_specs=None, out_specs=None, grid=(1,), scratch=(), aliases=None, us=0
):
    if in_specs is None:
        in_specs = [fixed(*o.shape) for o in operands]
    if out_specs is None:
        out_specs = [fixed(*o.shape) for o in out_shape]
    return pl.pallas_call(
        kernel,
        grid_spec=pltpu.PrefetchScalarGridSpec(
            num_scalar_prefetch=len(scalars), grid=grid, in_specs=in_specs, out_specs=out_specs, scratch_shapes=scratch
        ),
        out_shape=out_shape,
        compiler_params=pltpu.CompilerParams(vmem_limit_bytes=VMEM_LIMIT),
        input_output_aliases={len(scalars) + i: o for i, o in (aliases or {}).items()},
        cost_estimate=pl.CostEstimate(flops=1, bytes_accessed=max(1, us * 3000000), transcendentals=0),
        name=name,
    )(*scalars, *operands)


def piece_kernel(at, weight, bias, out):
    rows = out.shape[0] - PAD
    out[:rows, :] = weight[...]
    out[rows:, :] = jnp.broadcast_to(bias[...].astype(F32).reshape(1, -1), (PAD, out.shape[1])).astype(BF16)


def piece_call(at, weight, bias, rows):
    width = weight.shape[1]
    return call(
        piece_kernel,
        "weight_piece",
        (at,),
        (weight, bias),
        [like(rows + PAD, width)],
        in_specs=[pl.BlockSpec((rows, width), lambda i, s: (s[3], 0)), fixed(width)],
    )[0]


def count_kernel(base, slots, at, packed_ref, feat_ref, cot_ref, *refs):
    counts_ref, same_ref, other_ref, pack_ref, scale_ref = refs[-5:]
    rows = counts_ref.shape[0]
    step = pl.program_id(0)
    steps = pl.num_programs(0)
    block = (step + at[1] * (steps // 2)) % steps
    row = lax.broadcasted_iota(jnp.int32, (LANES, 8 * slots), 0)
    owner = lax.broadcasted_iota(jnp.int32, (1, 8 * slots), 1) // slots

    def group(index):
        entry = packed_ref[index : index + 1, :]
        high = (entry >> 7) * 8 + owner
        low = entry & (LANES - 1)
        left = jnp.where(high == row, 1.0, 0.0).astype(BF16)
        right = jnp.where(low == row, 1.0, 0.0).astype(BF16)
        return lax.dot_general(left, right, (((1,), (1,)), ((), ())), preferred_element_type=F32)

    for pair in range(rows // 16):
        first, second = group(2 * pair), group(2 * pair + 1)
        for tile in range(counts_ref.shape[1] // LANES):
            counts_ref[pair * 16 : (pair + 1) * 16, tile * LANES : (tile + 1) * LANES] = jnp.concatenate(
                [first[tile * 8 : (tile + 1) * 8], second[tile * 8 : (tile + 1) * 8]], 0
            ).astype(BF16)
    degree = jnp.sum(counts_ref[...].astype(F32), axis=1, keepdims=True)
    scale = 1.0 / (degree + 1.0)
    down = lax.broadcasted_iota(jnp.int32, (LANES, LANES), 0)
    across = lax.broadcasted_iota(jnp.int32, (LANES, LANES), 1)
    twice = jnp.where(down == across, 2.0, 0.0)
    column = pl.multiple_of(base + block * rows, LANES)
    tile_view = counts_ref[:, pl.ds(column, LANES)].astype(F32)
    counts_ref[:, pl.ds(column, LANES)] = (tile_view + twice).astype(BF16)
    total = jnp.dot(counts_ref[...], feat_ref[...], preferred_element_type=F32)
    result = (total * scale).astype(BF16)

    @pl.when(step < steps // 2)
    def _():
        same_ref[...] = result
        scale_ref[...] = scale

    @pl.when(step >= steps // 2)
    def _():
        other_ref[...] = result
        pack_ref[0] = result
        pack_ref[1] = cot_ref[...]


def count_call(at, packed, features, cotangent, base, size, counts):
    nodes, width = features.shape
    slots = packed.shape[1] // 8
    rows = LANES
    steps = size // rows
    half = steps // 2

    def natural(i, s):
        return base // rows + (i + s[1] * half) % steps

    def early(i, s):
        return jnp.minimum(i, half - 1), 0

    def late(i, s):
        return jnp.maximum(i - half, 0), 0

    operands = [packed, features, cotangent]
    specs = [
        pl.BlockSpec((rows // 8, 8 * slots), lambda i, s: (natural(i, s), 0)),
        fixed(nodes, width),
        pl.BlockSpec((rows, width), lambda i, s: (natural(i, s), 0)),
    ]
    aliases = {}
    if counts is not None:
        aliases = {len(operands): 0}
        operands.append(counts)
        specs.append(ANY)
    return call(
        functools.partial(count_kernel, base, slots),
        "count_and_aggregate",
        (at,),
        operands,
        [
            like(nodes, nodes),
            like(size // 2, width),
            like(size // 2, width),
            like(2, size // 2, width),
            like(size // 2, 1, dtype=F32),
        ],
        in_specs=specs,
        out_specs=[
            pl.BlockSpec((rows, nodes), lambda i, s: (natural(i, s), 0)),
            pl.BlockSpec((rows, width), early),
            pl.BlockSpec((rows, width), late),
            pl.BlockSpec((2, rows, width), lambda i, s: (0, *late(i, s))),
            pl.BlockSpec((rows, 1), early),
        ],
        grid=(steps,),
        aliases=aliases,
    )


def row_kernel(
    units, at, live, part0, near, part2, part3, scale, cot_own, weight_own, weight_sib, bias_own, bias_sib, *refs
):
    out_own, grads, back0, back_near, back2, back3 = refs[-6:]
    rows, width = part0.shape
    place = at[0]
    slot = (units[0] + at[1] * (units[1] - units[0])) * rows + lax.broadcasted_iota(jnp.int32, (rows, width), 0)
    living = slot < live[0]
    starts = [pl.multiple_of((place ^ code) * width, LANES) for code in range(4)]
    values = []
    for half, (weight, bias, cot) in enumerate(
        ((weight_own, bias_own, cot_own[...]), (weight_sib, bias_sib, near[1]))
    ):
        linear = bias[0:1, :].astype(F32)
        for part, start in zip((part0[...], near[0], part2[...], part3[...]), starts):
            linear = linear + jnp.dot(part, weight[pl.ds(start, width), :], preferred_element_type=F32)
        sigma = 1.0 / (1.0 + jnp.exp(-linear))
        result = jnp.where(living, linear * sigma, 0.0).astype(BF16)
        if half == 0:
            out_own[...] = result
        else:
            back_near[0] = result
        slope = sigma * (1.0 + linear * (1.0 - sigma))
        value = jnp.where(living, cot.astype(F32) * slope, 0.0).astype(BF16)
        grads[at[1] if half == 0 else 1 - at[1]] = value
        values.append(value)
    for code, start in enumerate(starts):
        total = jnp.zeros((rows, width), F32)
        for weight, value in zip((weight_own, weight_sib), values):
            total = total + lax.dot_general(
                value, weight[pl.ds(start, width), :], (((1,), (1,)), ((), ())), preferred_element_type=F32
            )
        total = (total * scale[...]).astype(BF16)
        if code == 1:
            back_near[1] = total
        else:
            (back0, None, back2, back3)[code][...] = total


def row_call(at, live, parts, scale, cotangent, weight_own, weight_sib, piece_own, piece_sib, entry, places, buffers):
    width = cotangent.shape[1]
    rows = cotangent.shape[0] // UNITS
    block, (low, high) = entry[1], units_of(entry)
    operands = [*parts, scale, cotangent, weight_own, weight_sib, piece_own, piece_sib]
    chunk = pl.BlockSpec((rows, width), lambda i, s, c: (block, 0))
    bias = pl.BlockSpec((PAD, width), lambda i, s, c: (piece_own.shape[0] // PAD - 1, 0))
    specs = [
        chunk,
        pl.BlockSpec((2, rows, width), lambda i, s, c: (0, block, 0)),
        chunk,
        chunk,
        pl.BlockSpec((rows, 1), lambda i, s, c: (block, 0)),
        pl.BlockSpec((rows, width), lambda i, s, c: (low + s[1] * (high - low), 0)),
        fixed(*weight_own.shape),
        fixed(*weight_sib.shape),
        bias,
        bias,
    ]
    shapes, outs, aliases = [], [], {}
    for number, (double, (index, length)) in enumerate(
        zip((False, True, False, True, False, False), (places[0],) * 4 + (places[1],) * 2)
    ):
        if double:
            shapes.append(like(2, length * rows, width))
            outs.append(pl.BlockSpec((2, rows, width), lambda i, s, c, index=index: (0, index, 0)))
        else:
            shapes.append(like(length * rows, width))
            outs.append(pl.BlockSpec((rows, width), lambda i, s, c, index=index: (index, 0)))
        if index > 0:
            aliases[len(operands)] = number
            operands.append(buffers[number])
            specs.append(ANY)
    return call(
        functools.partial(row_kernel, (low, high)),
        "linear_and_slope",
        (at, live),
        operands,
        shapes,
        in_specs=specs,
        out_specs=outs,
        aliases=aliases,
    )


def put_sums(ref, index, value):
    high = value.astype(BF16)
    low = (value - high.astype(F32)).astype(BF16)
    row = lax.broadcasted_iota(jnp.int32, (PAD, value.shape[1]), 0)
    both = jnp.where(row == 0, high.astype(F32), jnp.where(row == 1, low.astype(F32), 0.0))
    ref[(*index, slice(ref.shape[-2] - PAD, None), slice(None))] = both.astype(BF16)


def get_sums(ref, index):
    rows = ref[(*index, slice(ref.shape[-2] - PAD, None), slice(None))]
    return jnp.sum(rows.astype(F32), axis=0, keepdims=True)


def product_kernel(at, *refs):
    refs, terms = refs[:-1], refs[-1]
    parts, grads = refs[: -len(GROUPS)], refs[-len(GROUPS) :]
    unit = grads[0].shape[1] // len(PARTS[0])
    runs = []
    for group, entries in enumerate(PARTS):
        for index, (slab, block) in enumerate(entries):
            runs.append((slab, slice(block * unit, (block + 1) * unit), group, slice(index * unit, (index + 1) * unit)))
    width = parts[0].shape[-1]
    for half in range(2):
        for code in range(4):
            total = jnp.zeros((width, width), F32)
            for slab, from_rows, group, to_rows in runs:
                part = parts[4 * slab + code]
                part = part[0, from_rows, :] if code == 1 else part[from_rows, :]
                total = total + lax.dot_general(
                    part, grads[group][half, to_rows, :], (((0,), (0,)), ((), ())), preferred_element_type=F32
                )
            block = at[0] ^ code
            rows = pl.ds(pl.multiple_of((block % 2) * width, LANES), width)
            terms[block // 2, half, rows, :] = total.astype(BF16)
        sums = sum(jnp.sum(grad[half].astype(F32), axis=0, keepdims=True) for grad in grads)
        for side in range(2):
            put_sums(terms, (side, half), sums)


def product_call(at, parts, grads):
    width = grads[0].shape[-1]
    operands = [p for quad in parts for p in quad] + list(grads)
    return call(product_kernel, "weight_product", (at,), operands, [like(2, 2, 2 * width + PAD, width)])[0]


def fold_kernel(at, came, out):
    rows = out.shape[2] - PAD
    for half in range(2):
        sums = get_sums(came, (0, half)) + get_sums(came, (1, half))
        for part in range(2):
            low, high = part * rows, (part + 1) * rows
            total = came[0, half, low:high, :].astype(F32) + came[1, half, low:high, :].astype(F32)
            out[part, half, :rows, :] = total.astype(BF16)
            put_sums(out, (part, half), sums)


def fold_call(at, came):
    length, width = came.shape[2:]
    return call(fold_kernel, "fold_terms", (at,), (came,), [like(2, 2, (length - PAD) // 2 + PAD, width)])[0]


def part_kernel(at, came, out):
    rows = out.shape[1] - PAD
    for half in range(2):
        out[half, :rows, :] = (came[0, half, :rows, :].astype(F32) + came[1, half, :rows, :].astype(F32)).astype(BF16)
        put_sums(out, (half,), get_sums(came, (0, half)) + get_sums(came, (1, half)))


def part_call(at, came):
    return call(part_kernel, "part_terms", (at,), (came,), [like(*came.shape[1:])])[0]


def share_kernel(at, came, share, sums):
    rows = share.shape[0]
    share[...] = (came[0, :rows, :].astype(F32) + came[1, :rows, :].astype(F32)).astype(BF16)
    sums[...] = get_sums(came, (0,)) + get_sums(came, (1,))


def share_call(at, came):
    two, length, width = came.shape
    return call(
        share_kernel, "share_terms", (at,), (came,), [like(length - PAD, width), like(1, width, dtype=F32)]
    )


def join_kernel(stage, at, mine, theirs, out):
    rows = mine.shape[0]
    bit = (at[3] >> stage) % 2
    for copy in range(out.shape[0]):
        out[copy, pl.ds(pl.multiple_of(bit * rows, 16), rows), :] = mine[...]
        out[copy, pl.ds(pl.multiple_of((1 - bit) * rows, 16), rows), :] = theirs[...]


def join_call(at, stage, mine, theirs, copies):
    rows, width = mine.shape
    return call(
        functools.partial(join_kernel, stage), "join_halves", (at,), (mine, theirs), [like(copies, 2 * rows, width)]
    )[0]


def place_kernel(entries, at, mine, theirs, out):
    rows = mine.shape[0] // len(entries)
    for index, entry in enumerate(entries):
        low, high = units_of(entry)
        part = slice(index * rows, (index + 1) * rows)
        own = low + at[1] * (high - low)
        out[pl.ds(pl.multiple_of(own * rows, LANES), rows), :] = mine[part, :]
        out[pl.ds(pl.multiple_of((low + high - own) * rows, LANES), rows), :] = theirs[0, part, :]


def place_call(at, entries, mine, theirs):
    rows, width = mine.shape
    return call(
        functools.partial(place_kernel, entries),
        "place_rows",
        (at,),
        (mine, theirs),
        [like(rows // len(entries) * UNITS, width)],
        in_specs=[fixed(rows, width), fixed(1, rows, width)],
        us=3,
    )[0]


def spread_kernel(group, final, at, *refs):
    entries = PARTS[group]
    counts, refs = refs[: 2 * len(entries)], refs[2 * len(entries) :]
    (level, near), refs = refs[:2], refs[2:]
    fars, refs = refs[: 2 * len(GROUPS[group])], refs[2 * len(GROUPS[group]) :]
    scaled = refs[-1]
    rows = level.shape[0] // len(entries)
    step = pl.program_id(0)

    @pl.when(step == 0)
    def _():
        index = 0
        for run, entries in enumerate(GROUPS[group]):
            far, cross = fars[2 * run : 2 * run + 2]
            for number in range(len(entries)):
                part = slice(index * rows, (index + 1) * rows)
                there = slice(number * rows, (number + 1) * rows)
                scaled[2 * index + at[1]] = (level[part, :].astype(F32) + far[there, :].astype(F32)).astype(BF16)
                scaled[2 * index + 1 - at[1]] = (near[1, part, :].astype(F32) + cross[there, :].astype(F32)).astype(BF16)
                index += 1

    total = refs[0][...] if final else None
    for index, block in enumerate(counts):
        term = lax.dot_general(block[...], scaled[index], (((0,), (0,)), ((), ())), preferred_element_type=F32)
        total = term if total is None else total + term
    out = refs[3] if final else refs[0]
    out[...] = total.astype(out.dtype)
    if final:
        mine, output = refs[1], refs[4]
        half = pl.num_programs(0) // 2

        @pl.when(step // half == at[1])
        def _():
            output[...] = mine[...]

        @pl.when(step // half != at[1])
        def _():
            output[...] = near[0]


def spread_call(at, group, counts, level, near, fars, *last):
    nodes = counts.shape[0]
    rows, width = level.shape
    tile = 512
    final = len(last) > 0
    unit_rows = nodes // UNITS
    units = [unit for entry in PARTS[group] for unit in units_of(entry)]
    tiled = pl.BlockSpec((tile, width), lambda i, s: (i, 0))
    operands = [counts] * len(units) + [level, near, *fars, *last]
    specs = [pl.BlockSpec((unit_rows, tile), lambda i, s, unit=unit: (unit, i)) for unit in units]
    specs += [fixed(*o.shape) for o in (level, near, *fars)]
    shapes, outs, aliases = [like(nodes, width, dtype=F32)], [tiled], {}
    if final:
        (low, high), steps = units, nodes // tile
        specs += [tiled, fixed(rows, width), ANY]
        shapes = [like(nodes, width), like(nodes, width)]
        outs.append(pl.BlockSpec((unit_rows, width), lambda i, s: (jnp.where(i < steps // 2, low, high), 0)))
        aliases = {len(operands) - 1: 1}
    return call(
        functools.partial(spread_kernel, group, final),
        "spread_back",
        (at,),
        operands,
        shapes,
        in_specs=specs,
        out_specs=outs,
        grid=(nodes // tile,),
        scratch=[pltpu.VMEM((len(units), unit_rows, width), BF16)],
        aliases=aliases,
        us=8,
    )


def tie(value, *after):
    return lax.optimization_barrier((value, *after))[0]


def local(features, neighbour_lists, node_counts, weight, bias_terms, cotangent):
    dp_count = lax.axis_size("dp")
    mp_count = lax.axis_size("mp")
    bits = dp_count.bit_length() - 1
    place = lax.axis_index("mp")
    line = lax.axis_index("dp")
    core = line % 2
    nodes, width = features.shape
    depth = weight.shape[0]
    slots = neighbour_lists.shape[1]
    live = node_counts.astype(jnp.int32)
    orders = [(low, high) for low, high in zip(range(1, bits), range(bits - 1, 0, -1))] + [(0, 0)]
    piece_rows = depth // dp_count
    piece = jnp.int32(0)
    for stage, (low, high) in enumerate(orders):
        piece = piece + (jnp.where(core == 0, line >> low, line >> high) % 2 << stage)
    at = jnp.stack([place, place % 2, core, piece]).astype(jnp.int32)

    def across(value, code):
        return lax.ppermute(value, "mp", [(i, i ^ code) for i in range(mp_count)])

    def swap(value, stage):
        pairs = []
        for i in range(dp_count):
            bit = 1 << orders[stage][i % 2]
            if not i & bit:
                pairs.append([i, i | bit])
        return lax.all_to_all(value, "dp", 0, 0, axis_index_groups=pairs)

    def along(value, stage):
        return lax.ppermute(value, "dp", [(i, i ^ (1 << orders[stage][i % 2])) for i in range(dp_count)])

    def join_pieces(value):
        for stage in range(bits - 1):
            last = stage == bits - 2
            value = join_call(at, stage, value, along(value, stage), 2 if last else 1)
            value = value if last else value[0]
        return swap(value, bits - 1).reshape(-1, width)

    def gather_pieces(value):
        for stage in range(bits):
            value = swap(value, stage)
            value = value.reshape(-1, width)
            if stage < bits - 1:
                value = jnp.stack([value, value])
        return value

    unit = nodes // UNITS
    packed = neighbour_lists.reshape(nodes // 8, 8 * slots)
    piece_own = piece_call(at, weight, bias_terms, piece_rows)
    piece_sib = across(piece_own, 1)

    def count_slab(slab, counts):
        first, length = slab
        return count_call(tie(at, piece_own), packed, features, cotangent, first * unit, length * unit, counts)

    def zeros_for(function):
        return lambda *operands: jax.tree.map(
            lambda shape: jnp.zeros(shape.shape, shape.dtype), jax.eval_shape(function, *operands)
        )

    def always(function, *operands):
        return lax.cond(live[0] > 0, function, zeros_for(function), *operands)

    def last_rows(piece, counts):
        last = count_slab(SLABS[1], counts)
        return gather_pieces(jnp.stack([piece[:piece_rows]] * 2)), last

    counts, *first = count_slab(SLABS[0], None)
    same, other, pack, scale = (tie(value, piece_sib) for value in first)
    parts, scales = [(same, across(pack, 1), across(same, 2), across(other, 3))], [scale]
    weight_sib, (counts, same, other, pack, scale) = always(last_rows, piece_sib, counts)
    near, far, cross = parts[0][1:]
    parts.append(
        (same, across(tie(pack, cross), 1), across(tie(same, near), 2), across(tie(other, far), 3))
    )
    scales.append(scale)

    sides = []
    for group in GROUPS:
        total, index, buffers, runs = sum(map(len, group)), 0, None, []
        for run in group:
            for number, entry in enumerate(run):
                buffers = row_call(
                    at, live, parts[entry[0]], scales[entry[0]], cotangent, weight, weight_sib, piece_own, piece_sib,
                    entry, ((index, total), (number, len(run))), buffers,
                )
                index += 1
            runs.append(buffers[4:])
        sides.append((*buffers[:4], runs))
    grads = [side[1] for side in sides]

    def fold_terms(parts, grads):
        came = swap(product_call(at, parts, grads), bits - 1)
        for stage in range(bits - 2, -1, -1):
            came = swap(fold_call(at, came), stage)
        return part_call(at, came)

    def share_terms(came, counts, back, out_own):
        share, bias_grad = share_call(at, came)
        partial = spread_call(at, 0, counts, *back)[0]
        output = place_call(at, PARTS[0], out_own, back[1])
        return join_pieces(share).astype(F32), bias_grad, partial, output

    terms = always(fold_terms, parts, grads)
    backs = []
    for index, (_, _, level, near, runs) in enumerate(sides):
        if index == 1:
            mine = lax.dynamic_index_in_dim(terms, place % 2, 0, False)
            theirs = tie(lax.dynamic_index_in_dim(terms, 1 - place % 2, 0, False), backs[0][1], *backs[0][2])
            came = jnp.stack([mine, across(theirs, 1)])
            near = tie(near, came)
        fars = []
        for number, (far, cross) in enumerate(runs):
            if (index, number) == (0, 0):
                far, cross = tie(far, parts[-1][2]), tie(cross, parts[-1][2])
            if index == 1:
                far, cross = tie(far, theirs), tie(cross, theirs)
            fars += [across(far, 2), across(cross, 3)]
        backs.append((level, across(near, 1), fars))
    weight_grad, bias_grad, partial, output = always(share_terms, came, counts, backs[0], sides[0][0])
    features_grad, output = spread_call(at, 1, counts, *backs[1], partial, sides[1][0], output)
    return (output, features_grad, weight_grad, bias_grad.reshape(width))


def solution(mesh):
    in_specs = (P("dp", "mp"), P("dp", None), P("dp"), P(None, "mp"), P("mp"), P("dp", "mp"))
    out_specs = (P("dp", "mp"), P("dp", "mp"), P(None, "mp"), P("mp"))
    return jax.shard_map(local, mesh=mesh, in_specs=in_specs, out_specs=out_specs, check_vma=False)
```

```python
import functools

import jax
import jax.numpy as jnp
from jax import lax
from jax.experimental import pallas as pl
from jax.experimental.pallas import tpu as pltpu
from jax.sharding import PartitionSpec as P

BF16 = jnp.bfloat16
F32 = jnp.float32
UNITS = 8
SLABS = ((0, 4), (4, 4))
RUNS = (((0, 0),), ((0, 1), (1, 0)), ((1, 1),))
LANES = 128
PAD = 16
VMEM_LIMIT = 32 << 20
ANY = pl.BlockSpec(memory_space=pl.ANY)
HBM = pl.BlockSpec(memory_space=pltpu.HBM)


def like(*shape, dtype=BF16):
    return jax.ShapeDtypeStruct(shape, dtype)


def fixed(*shape):
    return pl.BlockSpec(shape, lambda *_: (0,) * len(shape))


def units_of(entry):
    slab, block = entry
    first, length = SLABS[slab]
    return first + block, first + length // 2 + block


def call(
    kernel, name, scalars, operands, out_shape, in_specs=None, out_specs=None, grid=(1,), scratch=(), aliases=None, us=0
):
    if in_specs is None:
        in_specs = [fixed(*o.shape) for o in operands]
    if out_specs is None:
        out_specs = [fixed(*o.shape) for o in out_shape]
    return pl.pallas_call(
        kernel,
        grid_spec=pltpu.PrefetchScalarGridSpec(
            num_scalar_prefetch=len(scalars), grid=grid, in_specs=in_specs, out_specs=out_specs, scratch_shapes=scratch
        ),
        out_shape=out_shape,
        compiler_params=pltpu.CompilerParams(vmem_limit_bytes=VMEM_LIMIT),
        input_output_aliases={len(scalars) + i: o for i, o in (aliases or {}).items()},
        cost_estimate=pl.CostEstimate(flops=1, bytes_accessed=max(1, us * 3000000), transcendentals=0),
        name=name,
    )(*scalars, *operands)


def piece_kernel(at, weight, bias, out, row, sems):
    rows = out.shape[0] - PAD
    copies = [
        pltpu.make_async_copy(weight.at[pl.ds(pl.multiple_of(at[3] * rows, 16), rows), :], out.at[:rows, :], sems.at[0]),
        pltpu.make_async_copy(bias, row, sems.at[1]),
    ]
    for copy in copies:
        copy.start()
    for copy in copies:
        copy.wait()
    out[rows:, :] = jnp.broadcast_to(row[...].astype(F32).reshape(1, -1), (PAD, out.shape[1])).astype(BF16)


def piece_call(at, weight, bias, rows):
    width = weight.shape[1]
    return call(
        piece_kernel,
        "weight_piece",
        (at,),
        (weight, bias),
        [like(rows + PAD, width)],
        in_specs=[HBM, HBM],
        scratch=[pltpu.VMEM((width,), BF16), pltpu.SemaphoreType.DMA((2,))],
    )[0]


def count_kernel(base, slots, at, packed_ref, feat_ref, cot_ref, *refs):
    counts_ref, same_ref, other_ref, pack_ref, scale_ref = refs[-5:]
    rows = counts_ref.shape[0]
    step = pl.program_id(0)
    steps = pl.num_programs(0)
    block = (step + at[1] * (steps // 2)) % steps
    lanes = 8 * slots
    row = lax.broadcasted_iota(jnp.int32, (LANES, lanes), 0).astype(F32).astype(BF16)
    owner = lax.broadcasted_iota(jnp.int32, (1, lanes), 1) // slots
    one, zero = jnp.ones((LANES, lanes), BF16), jnp.zeros((LANES, lanes), BF16)

    def one_hot(index):
        tile = jnp.broadcast_to(index.astype(F32), (16, lanes)).astype(BF16)
        return jnp.where(jnp.concatenate([tile] * (LANES // 16), 0) == row, one, zero)

    def group(index):
        entry = packed_ref[index : index + 1, :]
        left = one_hot((entry >> 7) * 8 + owner)
        right = one_hot(entry & (LANES - 1))
        return lax.dot_general(left, right, (((1,), (1,)), ((), ())), preferred_element_type=F32)

    for pair in range(rows // 16):
        first, second = group(2 * pair), group(2 * pair + 1)
        for tile in range(counts_ref.shape[1] // LANES):
            counts_ref[pair * 16 : (pair + 1) * 16, tile * LANES : (tile + 1) * LANES] = jnp.concatenate(
                [first[tile * 8 : (tile + 1) * 8], second[tile * 8 : (tile + 1) * 8]], 0
            ).astype(BF16)
    degree = jnp.sum(counts_ref[...].astype(F32), axis=1, keepdims=True)
    scale = 1.0 / (degree + 1.0)
    down = lax.broadcasted_iota(jnp.int32, (LANES, LANES), 0)
    across = lax.broadcasted_iota(jnp.int32, (LANES, LANES), 1)
    twice = jnp.where(down == across, 2.0, 0.0)
    for low in range(0, rows, LANES):
        where = slice(low, low + LANES), pl.ds(pl.multiple_of(base + block * rows + low, LANES), LANES)
        counts_ref[where] = (counts_ref[where].astype(F32) + twice).astype(BF16)
    total = jnp.dot(counts_ref[...], feat_ref[...], preferred_element_type=F32)
    result = (total * scale).astype(BF16)

    @pl.when(step < steps // 2)
    def _():
        same_ref[...] = result
        scale_ref[...] = scale

    @pl.when(step >= steps // 2)
    def _():
        other_ref[...] = result
        pack_ref[0] = result
        pack_ref[1] = cot_ref[...]


def count_call(at, packed, features, cotangent, base, size, counts):
    nodes, width = features.shape
    slots = packed.shape[1] // 8
    rows = 2 * LANES
    steps = size // rows
    half = steps // 2

    def natural(i, s):
        return base // rows + (i + s[1] * half) % steps

    def early(i, s):
        return jnp.minimum(i, half - 1), 0

    def late(i, s):
        return jnp.maximum(i - half, 0), 0

    operands = [packed, features, cotangent]
    specs = [
        pl.BlockSpec((rows // 8, 8 * slots), lambda i, s: (natural(i, s), 0)),
        fixed(nodes, width),
        pl.BlockSpec((rows, width), lambda i, s: (natural(i, s), 0)),
    ]
    aliases = {}
    if counts is not None:
        aliases = {len(operands): 0}
        operands.append(counts)
        specs.append(ANY)
    return call(
        functools.partial(count_kernel, base, slots),
        "count_and_aggregate",
        (at,),
        operands,
        [
            like(nodes, nodes),
            like(size // 2, width),
            like(size // 2, width),
            like(2, size // 2, width),
            like(size // 2, 1, dtype=F32),
        ],
        in_specs=specs,
        out_specs=[
            pl.BlockSpec((rows, nodes), lambda i, s: (natural(i, s), 0)),
            pl.BlockSpec((rows, width), early),
            pl.BlockSpec((rows, width), late),
            pl.BlockSpec((2, rows, width), lambda i, s: (0, *late(i, s))),
            pl.BlockSpec((rows, 1), early),
        ],
        grid=(steps,),
        aliases=aliases,
    )


def row_kernel(
    units, at, live, part0, near, part2, part3, scale, cot_own, weight_own, weight_sib, bias_own, bias_sib, *refs
):
    out_own, grads, back0, back_near, back2, back3 = refs[-6:]
    rows, width = part0.shape
    place = at[0]
    slot = (units[0] + at[1] * (units[1] - units[0])) * rows + lax.broadcasted_iota(jnp.int32, (rows, width), 0)
    living = slot < live[0]
    starts = [pl.multiple_of((place ^ code) * width, LANES) for code in range(4)]
    values = []
    for half, (weight, bias, cot) in enumerate(
        ((weight_own, bias_own, cot_own[...]), (weight_sib, bias_sib, near[1]))
    ):
        linear = bias[0:1, :].astype(F32)
        for part, start in zip((part0[...], near[0], part2[...], part3[...]), starts):
            linear = linear + jnp.dot(part, weight[pl.ds(start, width), :], preferred_element_type=F32)
        sigma = 1.0 / (1.0 + jnp.exp(-linear))
        result = jnp.where(living, linear * sigma, 0.0).astype(BF16)
        if half == 0:
            out_own[...] = result
        else:
            back_near[0] = result
        slope = sigma * (1.0 + linear * (1.0 - sigma))
        value = jnp.where(living, cot.astype(F32) * slope, 0.0).astype(BF16)
        grads[at[1] if half == 0 else 1 - at[1]] = value
        values.append(value)
    for code, start in enumerate(starts):
        total = jnp.zeros((rows, width), F32)
        for weight, value in zip((weight_own, weight_sib), values):
            total = total + lax.dot_general(
                value, weight[pl.ds(start, width), :], (((1,), (1,)), ((), ())), preferred_element_type=F32
            )
        total = (total * scale[...]).astype(BF16)
        if code == 1:
            back_near[1] = total
        else:
            (back0, None, back2, back3)[code][...] = total


def row_call(
    at, live, parts, scale, cotangent, weight_own, weight_sib, piece_own, piece_sib, entry, index, length, buffers
):
    width = cotangent.shape[1]
    rows = cotangent.shape[0] // UNITS
    block, (low, high) = entry[1], units_of(entry)
    operands = [*parts, scale, cotangent, weight_own, weight_sib, piece_own, piece_sib]
    chunk = pl.BlockSpec((rows, width), lambda i, s, c: (block, 0))
    bias = pl.BlockSpec((PAD, width), lambda i, s, c: (piece_own.shape[0] // PAD - 1, 0))
    specs = [
        chunk,
        pl.BlockSpec((2, rows, width), lambda i, s, c: (0, block, 0)),
        chunk,
        chunk,
        pl.BlockSpec((rows, 1), lambda i, s, c: (block, 0)),
        pl.BlockSpec((rows, width), lambda i, s, c: (low + s[1] * (high - low), 0)),
        fixed(*weight_own.shape),
        fixed(*weight_sib.shape),
        bias,
        bias,
    ]
    shapes, outs, aliases = [], [], {}
    for number, double in enumerate((False, True, False, True, False, False)):
        if double:
            shapes.append(like(2, length * rows, width))
            outs.append(pl.BlockSpec((2, rows, width), lambda i, s, c: (0, index, 0)))
        else:
            shapes.append(like(length * rows, width))
            outs.append(pl.BlockSpec((rows, width), lambda i, s, c: (index, 0)))
        if index > 0:
            aliases[len(operands)] = number
            operands.append(buffers[number])
            specs.append(ANY)
    return call(
        functools.partial(row_kernel, (low, high)),
        "linear_and_slope",
        (at, live),
        operands,
        shapes,
        in_specs=specs,
        out_specs=outs,
        aliases=aliases,
    )


def put_sums(ref, index, value):
    high = value.astype(BF16)
    low = (value - high.astype(F32)).astype(BF16)
    row = lax.broadcasted_iota(jnp.int32, (PAD, value.shape[1]), 0)
    both = jnp.where(row == 0, high.astype(F32), jnp.where(row == 1, low.astype(F32), 0.0))
    ref[(*index, slice(ref.shape[-2] - PAD, None), slice(None))] = both.astype(BF16)


def get_sums(ref, index):
    rows = ref[(*index, slice(ref.shape[-2] - PAD, None), slice(None))]
    return jnp.sum(rows.astype(F32), axis=0, keepdims=True)


def product_kernel(at, *refs):
    refs, terms = refs[:-1], refs[-1]
    parts, grads = refs[: -len(RUNS)], refs[-len(RUNS) :]
    unit = grads[0].shape[1] // len(RUNS[0])
    runs = []
    for group, entries in enumerate(RUNS):
        for index, (slab, block) in enumerate(entries):
            runs.append((slab, slice(block * unit, (block + 1) * unit), group, slice(index * unit, (index + 1) * unit)))
    width = parts[0].shape[-1]
    for half in range(2):
        for code in range(4):
            total = jnp.zeros((width, width), F32)
            for slab, from_rows, group, to_rows in runs:
                part = parts[4 * slab + code]
                part = part[0, from_rows, :] if code == 1 else part[from_rows, :]
                total = total + lax.dot_general(
                    part, grads[group][half, to_rows, :], (((0,), (0,)), ((), ())), preferred_element_type=F32
                )
            block = at[0] ^ code
            rows = pl.ds(pl.multiple_of((block % 2) * width, LANES), width)
            terms[block // 2, half, rows, :] = total.astype(BF16)
        sums = sum(jnp.sum(grad[half].astype(F32), axis=0, keepdims=True) for grad in grads)
        for side in range(2):
            put_sums(terms, (side, half), sums)


def product_call(at, parts, grads):
    width = grads[0].shape[-1]
    operands = [p for quad in parts for p in quad] + list(grads)
    return call(product_kernel, "weight_product", (at,), operands, [like(2, 2, 2 * width + PAD, width)])[0]


def pair_of(refs):
    return [refs[0].at[0], refs[0].at[1]] if len(refs) == 1 else list(refs)


def fold_kernel(stage, at, *refs):
    first, second = pair_of(refs[:-2])
    keep, give = refs[-2:]
    rows = keep.shape[1] - PAD
    bit = (at[3] >> stage) % 2
    for half in range(2):
        sums = get_sums(first, (half,)) + get_sums(second, (half,))
        for out, part in ((keep, bit), (give, 1 - bit)):
            where = pl.ds(pl.multiple_of(part * rows, 16), rows)
            out[half, :rows, :] = (first[half, where, :].astype(F32) + second[half, where, :].astype(F32)).astype(BF16)
            put_sums(out, (half,), sums)


def fold_call(at, stage, operands):
    length, width = operands[0].shape[-2:]
    shape = like(2, (length - PAD) // 2 + PAD, width)
    return call(functools.partial(fold_kernel, stage), "fold_terms", (at,), operands, [shape, shape])


def part_kernel(at, *refs):
    first, second = pair_of(refs[:-1])
    out = refs[-1]
    rows = out.shape[1] - PAD
    for half in range(2):
        out[half, :rows, :] = (first[half, :rows, :].astype(F32) + second[half, :rows, :].astype(F32)).astype(BF16)
        put_sums(out, (half,), get_sums(first, (half,)) + get_sums(second, (half,)))


def part_call(at, operands):
    return call(part_kernel, "part_terms", (at,), operands, [like(*operands[0].shape[-3:])])[0]


def share_kernel(at, came, share, sums):
    rows = share.shape[0]
    share[...] = (came[0, :rows, :].astype(F32) + came[1, :rows, :].astype(F32)).astype(BF16)
    sums[...] = get_sums(came, (0,)) + get_sums(came, (1,))


def share_call(at, came):
    two, length, width = came.shape
    return call(
        share_kernel, "share_terms", (at,), (came,), [like(length - PAD, width), like(1, width, dtype=F32)]
    )


def join_kernel(stage, at, mine, theirs, out):
    rows = mine.shape[0]
    bit = (at[3] >> stage) % 2
    for copy in range(out.shape[0]):
        out[copy, pl.ds(pl.multiple_of(bit * rows, 16), rows), :] = mine[...]
        out[copy, pl.ds(pl.multiple_of((1 - bit) * rows, 16), rows), :] = theirs[...]


def join_call(at, stage, mine, theirs, copies):
    rows, width = mine.shape
    return call(
        functools.partial(join_kernel, stage), "join_halves", (at,), (mine, theirs), [like(copies, 2 * rows, width)]
    )[0]


def place_kernel(runs, at, *refs):
    out = refs[-1]
    for run, mine, theirs in zip(runs, refs[0:-1:2], refs[1:-1:2]):
        rows = mine.shape[0] // len(run)
        for index, entry in enumerate(run):
            low, high = units_of(entry)
            part = slice(index * rows, (index + 1) * rows)
            own = low + at[1] * (high - low)
            out[pl.ds(pl.multiple_of(own * rows, LANES), rows), :] = mine[part, :]
            out[pl.ds(pl.multiple_of((low + high - own) * rows, LANES), rows), :] = theirs[0, part, :]


def place_call(at, runs, pairs):
    rows, width = pairs[0][0].shape
    specs = [spec for mine, _ in pairs for spec in (fixed(*mine.shape), fixed(1, *mine.shape))]
    return call(
        functools.partial(place_kernel, runs),
        "place_rows",
        (at,),
        [o for pair in pairs for o in pair],
        [pltpu.HBM((rows // len(runs[0]) * UNITS, width), BF16)],
        in_specs=specs,
        us=3,
    )[0]


def spread_kernel(runs, final, at, *refs):
    units = 2 * sum(map(len, runs))
    counts, backs, refs = refs[:units], refs[units : units + 4 * len(runs)], refs[units + 4 * len(runs) :]
    scaled = refs[-1]
    step = pl.program_id(0)

    @pl.when(step == 0)
    def _():
        at_unit = 0
        for number, run in enumerate(runs):
            level, near, far, cross = backs[4 * number : 4 * number + 4]
            rows = level.shape[0] // len(run)
            for index in range(len(run)):
                part = slice(index * rows, (index + 1) * rows)
                scaled[at_unit + at[1]] = (level[part, :].astype(F32) + far[part, :].astype(F32)).astype(BF16)
                scaled[at_unit + 1 - at[1]] = (near[1, part, :].astype(F32) + cross[part, :].astype(F32)).astype(BF16)
                at_unit += 2

    total = refs[0][...] if final else None
    for index, block in enumerate(counts):
        term = lax.dot_general(block[...], scaled[index], (((0,), (0,)), ((), ())), preferred_element_type=F32)
        total = term if total is None else total + term
    out = refs[3] if final else refs[0]
    out[...] = total.astype(out.dtype)
    if final:
        mine, output, near = refs[1], refs[4], backs[1]
        half = pl.num_programs(0) // 2

        @pl.when(step // half == at[1])
        def _():
            output[...] = mine[...]

        @pl.when(step // half != at[1])
        def _():
            output[...] = near[0]


def spread_call(at, runs, counts, backs, *last):
    nodes = counts.shape[0]
    width = backs[0].shape[1]
    tile = 512
    final = len(last) > 0
    unit_rows = nodes // UNITS
    units = [unit for run in runs for entry in run for unit in units_of(entry)]
    tiled = pl.BlockSpec((tile, width), lambda i, s: (i, 0))
    operands = [counts] * len(units) + [*backs, *last]
    specs = [pl.BlockSpec((unit_rows, tile), lambda i, s, unit=unit: (unit, i)) for unit in units]
    specs += [fixed(*o.shape) for o in backs]
    shapes, outs, aliases = [like(nodes, width, dtype=F32)], [tiled], {}
    if final:
        (low, high), steps = units, nodes // tile
        specs += [tiled, fixed(unit_rows, width), ANY]
        shapes = [pltpu.HBM((nodes, width), BF16), pltpu.HBM((nodes, width), BF16)]
        outs.append(pl.BlockSpec((unit_rows, width), lambda i, s: (jnp.where(i < steps // 2, low, high), 0)))
        aliases = {len(operands) - 1: 1}
    return call(
        functools.partial(spread_kernel, runs, final),
        "spread_back",
        (at,),
        operands,
        shapes,
        in_specs=specs,
        out_specs=outs,
        grid=(nodes // tile,),
        scratch=[pltpu.VMEM((len(units), unit_rows, width), BF16)],
        aliases=aliases,
        us=8,
    )


def tie(value, *after):
    return lax.optimization_barrier((value, *after))[0]


def local(features, neighbour_lists, node_counts, weight, bias_terms, cotangent):
    dp_count = lax.axis_size("dp")
    mp_count = lax.axis_size("mp")
    bits = dp_count.bit_length() - 1
    place = lax.axis_index("mp")
    line = lax.axis_index("dp")
    core = line % 2
    nodes, width = features.shape
    depth = weight.shape[0]
    slots = neighbour_lists.shape[1]
    live = node_counts.astype(jnp.int32)
    orders = [(low, high) for low, high in zip(range(1, bits), range(bits - 1, 0, -1))] + [(0, 0)]
    piece_rows = depth // dp_count
    piece = jnp.int32(0)
    for stage, (low, high) in enumerate(orders):
        piece = piece + (jnp.where(core == 0, line >> low, line >> high) % 2 << stage)
    at = jnp.stack([place, place % 2, core, piece]).astype(jnp.int32)

    def across(value, code):
        return lax.ppermute(value, "mp", [(i, i ^ code) for i in range(mp_count)])

    def swap(value, stage):
        pairs = []
        for i in range(dp_count):
            bit = 1 << orders[stage][i % 2]
            if not i & bit:
                pairs.append([i, i | bit])
        return lax.all_to_all(value, "dp", 0, 0, axis_index_groups=pairs)

    def along(value, stage):
        return lax.ppermute(value, "dp", [(i, i ^ (1 << orders[stage][i % 2])) for i in range(dp_count)])

    def join_pieces(value, first):
        for stage in range(bits - 1):
            last = stage == bits - 2
            came = along(value, stage)
            if stage == 0:
                came = tie(came, first)
            value = join_call(at, stage, value, came, 2 if last else 1)
            value = value if last else value[0]
        return swap(value, bits - 1).reshape(-1, width)

    unit = nodes // UNITS
    packed = neighbour_lists.reshape(nodes // 8, 8 * slots)
    piece_own = piece_call(at, weight, bias_terms, piece_rows)
    piece_sib = across(piece_own, 1)

    def count_slab(slab, counts):
        first, length = slab
        return count_call(tie(at, piece_own), packed, features, cotangent, first * unit, length * unit, counts)

    def zeros_for(function):
        return lambda *operands: jax.tree.map(
            lambda shape: jnp.zeros(shape.shape, shape.dtype), jax.eval_shape(function, *operands)
        )

    def always(function, *operands):
        return lax.cond(live[0] > 0, function, zeros_for(function), *operands)

    def last_rows(piece, counts):
        last = count_slab(SLABS[1], counts)
        return join_pieces(piece[:piece_rows], last[1]), last

    counts, *first = count_slab(SLABS[0], None)
    same, other, pack, scale = (tie(value, piece_sib) for value in first)
    parts, scales = [(same, across(pack, 1), across(same, 2), across(other, 3))], [scale]
    weight_sib, (counts, same, other, pack, scale) = always(last_rows, piece_sib, counts)
    near, far, cross = parts[0][1:]
    parts.append(
        (same, across(tie(pack, cross), 1), across(tie(same, near), 2), across(tie(other, far), 3))
    )
    scales.append(scale)

    sides = []
    for run in RUNS:
        buffers = None
        for index, entry in enumerate(run):
            buffers = row_call(
                at, live, parts[entry[0]], scales[entry[0]], cotangent, weight, weight_sib, piece_own, piece_sib,
                entry, index, len(run), buffers,
            )
        sides.append(buffers)
    grads = [side[1] for side in sides]

    def fold_terms(parts, grads):
        pair = (swap(product_call(at, parts, grads), bits - 1),)
        for stage in range(bits - 2, -1, -1):
            keep, give = fold_call(at, stage, pair)
            pair = (keep, along(give, stage))
        return part_call(at, pair)

    def share_terms(came, counts, backs, outs):
        share, bias_grad = share_call(at, came)
        output = place_call(at, RUNS[:-1], [(out, back[1]) for out, back in zip(outs, backs)])
        partial = spread_call(at, RUNS[:-1], counts, [o for back in backs for o in back])[0]
        return join_pieces(share, output).astype(F32), bias_grad, partial, output

    backs = []
    for index, (_, _, level, near, far, cross) in enumerate(sides):
        if index == 0:
            far, cross, near = tie(far, parts[-1][2]), tie(cross, parts[-1][2]), tie(near, parts[-1][3])
        if index == 1:
            terms = always(fold_terms, parts, [tie(grad, *backs[0][1:]) for grad in grads])
            near = tie(near, *backs[0][1:], grads[-1])
        if index == 2:
            mine = lax.dynamic_index_in_dim(terms, place % 2, 0, False)
            theirs = lax.dynamic_index_in_dim(terms, 1 - place % 2, 0, False)
            theirs = tie(theirs, *backs[0][1:], *backs[1][1:])
            came = jnp.stack([mine, across(theirs, 1)])
            near, far, cross = tie(near, came), tie(far, theirs), tie(cross, theirs)
        backs.append((level, across(near, 1), across(far, 2), across(cross, 3)))
    outs = [side[0] for side in sides]
    weight_grad, bias_grad, partial, output = always(share_terms, came, counts, backs[:-1], outs[:-1])
    features_grad, output = spread_call(at, RUNS[-1:], counts, backs[-1], partial, outs[-1], output)
    return (output, features_grad, weight_grad, bias_grad.reshape(width))


def solution(mesh):
    in_specs = (P("dp", "mp"), P("dp", None), P("dp"), P(None, "mp"), P("mp"), P("dp", "mp"))
    out_specs = (P("dp", "mp"), P("dp", "mp"), P(None, "mp"), P("mp"))
    return jax.shard_map(local, mesh=mesh, in_specs=in_specs, out_specs=out_specs, check_vma=False)
```

```python
import functools

import jax
import jax.numpy as jnp
from jax import lax
from jax.experimental import pallas as pl
from jax.experimental.pallas import tpu as pltpu
from jax.sharding import PartitionSpec as P

BF16 = jnp.bfloat16
F32 = jnp.float32
UNITS = 8
SLABS = ((0, 4), (4, 4))
RUNS = (((0, 0),), ((0, 1), (1, 0)), ((1, 1),))
LANES = 128
PAD = 16
VMEM_LIMIT = 32 << 20
ANY = pl.BlockSpec(memory_space=pl.ANY)
HBM = pl.BlockSpec(memory_space=pltpu.HBM)


def like(*shape, dtype=BF16):
    return jax.ShapeDtypeStruct(shape, dtype)


def fixed(*shape):
    return pl.BlockSpec(shape, lambda *_: (0,) * len(shape))


def units_of(entry):
    slab, block = entry
    first, length = SLABS[slab]
    return first + block, first + length // 2 + block


def call(
    kernel, name, scalars, operands, out_shape, in_specs=None, out_specs=None, grid=(1,), scratch=(), aliases=None, us=0
):
    if in_specs is None:
        in_specs = [fixed(*o.shape) for o in operands]
    if out_specs is None:
        out_specs = [fixed(*o.shape) for o in out_shape]
    return pl.pallas_call(
        kernel,
        grid_spec=pltpu.PrefetchScalarGridSpec(
            num_scalar_prefetch=len(scalars), grid=grid, in_specs=in_specs, out_specs=out_specs, scratch_shapes=scratch
        ),
        out_shape=out_shape,
        compiler_params=pltpu.CompilerParams(vmem_limit_bytes=VMEM_LIMIT),
        input_output_aliases={len(scalars) + i: o for i, o in (aliases or {}).items()},
        cost_estimate=pl.CostEstimate(flops=1, bytes_accessed=max(1, us * 3000000), transcendentals=0),
        name=name,
    )(*scalars, *operands)


def piece_kernel(at, weight, bias, out, row, sems):
    rows = out.shape[0] - PAD
    copies = [
        pltpu.make_async_copy(weight.at[pl.ds(pl.multiple_of(at[3] * rows, 16), rows), :], out.at[:rows, :], sems.at[0]),
        pltpu.make_async_copy(bias, row, sems.at[1]),
    ]
    for copy in copies:
        copy.start()
    for copy in copies:
        copy.wait()
    out[rows:, :] = jnp.broadcast_to(row[...].astype(F32).reshape(1, -1), (PAD, out.shape[1])).astype(BF16)


def piece_call(at, weight, bias, rows):
    width = weight.shape[1]
    return call(
        piece_kernel,
        "weight_piece",
        (at,),
        [pltpu.with_memory_space_constraint(value, pltpu.HBM) for value in (weight, bias)],
        [like(rows + PAD, width)],
        in_specs=[HBM, HBM],
        scratch=[pltpu.VMEM((width,), BF16), pltpu.SemaphoreType.DMA((2,))],
    )[0]


def count_kernel(base, slots, at, packed_ref, feat_ref, cot_ref, *refs):
    counts_ref, same_ref, other_ref, pack_ref, scale_ref = refs[-5:]
    rows = counts_ref.shape[0]
    step = pl.program_id(0)
    steps = pl.num_programs(0)
    block = (step + at[1] * (steps // 2)) % steps
    lanes = 8 * slots
    row = lax.broadcasted_iota(jnp.int32, (LANES, lanes), 0).astype(F32).astype(BF16)
    owner = lax.broadcasted_iota(jnp.int32, (1, lanes), 1) // slots
    one, zero = jnp.ones((LANES, lanes), BF16), jnp.zeros((LANES, lanes), BF16)

    def one_hot(index):
        tile = jnp.broadcast_to(index.astype(F32), (16, lanes)).astype(BF16)
        return jnp.where(jnp.concatenate([tile] * (LANES // 16), 0) == row, one, zero)

    def group(index):
        entry = packed_ref[index : index + 1, :]
        left = one_hot((entry >> 7) * 8 + owner)
        right = one_hot(entry & (LANES - 1))
        return lax.dot_general(left, right, (((1,), (1,)), ((), ())), preferred_element_type=F32)

    for pair in range(rows // 16):
        first, second = group(2 * pair), group(2 * pair + 1)
        for tile in range(counts_ref.shape[1] // LANES):
            counts_ref[pair * 16 : (pair + 1) * 16, tile * LANES : (tile + 1) * LANES] = jnp.concatenate(
                [first[tile * 8 : (tile + 1) * 8], second[tile * 8 : (tile + 1) * 8]], 0
            ).astype(BF16)
    degree = jnp.sum(counts_ref[...].astype(F32), axis=1, keepdims=True)
    scale = 1.0 / (degree + 1.0)
    down = lax.broadcasted_iota(jnp.int32, (LANES, LANES), 0)
    across = lax.broadcasted_iota(jnp.int32, (LANES, LANES), 1)
    twice = jnp.where(down == across, 2.0, 0.0)
    for low in range(0, rows, LANES):
        where = slice(low, low + LANES), pl.ds(pl.multiple_of(base + block * rows + low, LANES), LANES)
        counts_ref[where] = (counts_ref[where].astype(F32) + twice).astype(BF16)
    total = jnp.dot(counts_ref[...], feat_ref[...], preferred_element_type=F32)
    result = (total * scale).astype(BF16)

    @pl.when(step < steps // 2)
    def _():
        same_ref[...] = result
        scale_ref[...] = scale

    @pl.when(step >= steps // 2)
    def _():
        other_ref[...] = result
        pack_ref[0] = result
        pack_ref[1] = cot_ref[...]


def count_call(at, packed, features, cotangent, base, size, counts):
    nodes, width = features.shape
    slots = packed.shape[1] // 8
    rows = 2 * LANES
    steps = size // rows
    half = steps // 2

    def natural(i, s):
        return base // rows + (i + s[1] * half) % steps

    def early(i, s):
        return jnp.minimum(i, half - 1), 0

    def late(i, s):
        return jnp.maximum(i - half, 0), 0

    operands = [packed, features, cotangent]
    specs = [
        pl.BlockSpec((rows // 8, 8 * slots), lambda i, s: (natural(i, s), 0)),
        fixed(nodes, width),
        pl.BlockSpec((rows, width), lambda i, s: (natural(i, s), 0)),
    ]
    aliases = {}
    if counts is not None:
        aliases = {len(operands): 0}
        operands.append(counts)
        specs.append(ANY)
    return call(
        functools.partial(count_kernel, base, slots),
        "count_and_aggregate",
        (at,),
        operands,
        [
            like(nodes, nodes),
            like(size // 2, width),
            like(size // 2, width),
            like(2, size // 2, width),
            like(size // 2, 1, dtype=F32),
        ],
        in_specs=specs,
        out_specs=[
            pl.BlockSpec((rows, nodes), lambda i, s: (natural(i, s), 0)),
            pl.BlockSpec((rows, width), early),
            pl.BlockSpec((rows, width), late),
            pl.BlockSpec((2, rows, width), lambda i, s: (0, *late(i, s))),
            pl.BlockSpec((rows, 1), early),
        ],
        grid=(steps,),
        aliases=aliases,
    )


def row_kernel(
    units, at, live, part0, near, part2, part3, scale, cot_own, weight_own, weight_sib, bias_own, bias_sib, *refs
):
    out_own, grads, back0, back_near, back2, back3 = refs[-6:]
    rows, width = part0.shape
    place = at[0]
    slot = (units[0] + at[1] * (units[1] - units[0])) * rows + lax.broadcasted_iota(jnp.int32, (rows, width), 0)
    living = slot < live[0]
    starts = [pl.multiple_of((place ^ code) * width, LANES) for code in range(4)]
    values = []
    for half, (weight, bias, cot) in enumerate(
        ((weight_own, bias_own, cot_own[...]), (weight_sib, bias_sib, near[1]))
    ):
        linear = bias[0:1, :].astype(F32)
        for part, start in zip((part0[...], near[0], part2[...], part3[...]), starts):
            linear = linear + jnp.dot(part, weight[pl.ds(start, width), :], preferred_element_type=F32)
        sigma = 1.0 / (1.0 + jnp.exp(-linear))
        result = jnp.where(living, linear * sigma, 0.0).astype(BF16)
        if half == 0:
            out_own[...] = result
        else:
            back_near[0] = result
        slope = sigma * (1.0 + linear * (1.0 - sigma))
        value = jnp.where(living, cot.astype(F32) * slope, 0.0).astype(BF16)
        grads[at[1] if half == 0 else 1 - at[1]] = value
        values.append(value)
    for code, start in enumerate(starts):
        total = jnp.zeros((rows, width), F32)
        for weight, value in zip((weight_own, weight_sib), values):
            total = total + lax.dot_general(
                value, weight[pl.ds(start, width), :], (((1,), (1,)), ((), ())), preferred_element_type=F32
            )
        total = (total * scale[...]).astype(BF16)
        if code == 1:
            back_near[1] = total
        else:
            (back0, None, back2, back3)[code][...] = total


def row_call(
    at, live, parts, scale, cotangent, weight_own, weight_sib, piece_own, piece_sib, entry, index, length, buffers
):
    width = cotangent.shape[1]
    rows = cotangent.shape[0] // UNITS
    block, (low, high) = entry[1], units_of(entry)
    operands = [*parts, scale, cotangent, weight_own, weight_sib, piece_own, piece_sib]
    chunk = pl.BlockSpec((rows, width), lambda i, s, c: (block, 0))
    bias = pl.BlockSpec((PAD, width), lambda i, s, c: (piece_own.shape[0] // PAD - 1, 0))
    specs = [
        chunk,
        pl.BlockSpec((2, rows, width), lambda i, s, c: (0, block, 0)),
        chunk,
        chunk,
        pl.BlockSpec((rows, 1), lambda i, s, c: (block, 0)),
        pl.BlockSpec((rows, width), lambda i, s, c: (low + s[1] * (high - low), 0)),
        fixed(*weight_own.shape),
        fixed(*weight_sib.shape),
        bias,
        bias,
    ]
    shapes, outs, aliases = [], [], {}
    for number, double in enumerate((False, True, False, True, False, False)):
        if double:
            shapes.append(like(2, length * rows, width))
            outs.append(pl.BlockSpec((2, rows, width), lambda i, s, c: (0, index, 0)))
        else:
            shapes.append(like(length * rows, width))
            outs.append(pl.BlockSpec((rows, width), lambda i, s, c: (index, 0)))
        if index > 0:
            aliases[len(operands)] = number
            operands.append(buffers[number])
            specs.append(ANY)
    return call(
        functools.partial(row_kernel, (low, high)),
        "linear_and_slope",
        (at, live),
        operands,
        shapes,
        in_specs=specs,
        out_specs=outs,
        aliases=aliases,
    )


def put_sums(ref, index, value):
    high = value.astype(BF16)
    low = (value - high.astype(F32)).astype(BF16)
    row = lax.broadcasted_iota(jnp.int32, (PAD, value.shape[1]), 0)
    both = jnp.where(row == 0, high.astype(F32), jnp.where(row == 1, low.astype(F32), 0.0))
    ref[(*index, slice(ref.shape[-2] - PAD, None), slice(None))] = both.astype(BF16)


def get_sums(ref, index):
    rows = ref[(*index, slice(ref.shape[-2] - PAD, None), slice(None))]
    return jnp.sum(rows.astype(F32), axis=0, keepdims=True)


def product_kernel(at, *refs):
    refs, terms = refs[:-1], refs[-1]
    parts, grads = refs[: -len(RUNS)], refs[-len(RUNS) :]
    unit = grads[0].shape[1] // len(RUNS[0])
    runs = []
    for group, entries in enumerate(RUNS):
        for index, (slab, block) in enumerate(entries):
            runs.append((slab, slice(block * unit, (block + 1) * unit), group, slice(index * unit, (index + 1) * unit)))
    width = parts[0].shape[-1]
    for half in range(2):
        for code in range(4):
            total = jnp.zeros((width, width), F32)
            for slab, from_rows, group, to_rows in runs:
                part = parts[4 * slab + code]
                part = part[0, from_rows, :] if code == 1 else part[from_rows, :]
                total = total + lax.dot_general(
                    part, grads[group][half, to_rows, :], (((0,), (0,)), ((), ())), preferred_element_type=F32
                )
            block = at[0] ^ code
            rows = pl.ds(pl.multiple_of((block % 2) * width, LANES), width)
            terms[block // 2, half, rows, :] = total.astype(BF16)
        sums = sum(jnp.sum(grad[half].astype(F32), axis=0, keepdims=True) for grad in grads)
        for side in range(2):
            put_sums(terms, (side, half), sums)


def product_call(at, parts, grads):
    width = grads[0].shape[-1]
    operands = [p for quad in parts for p in quad] + list(grads)
    return call(product_kernel, "weight_product", (at,), operands, [like(2, 2, 2 * width + PAD, width)])[0]


def pair_of(refs):
    return [refs[0].at[0], refs[0].at[1]] if len(refs) == 1 else list(refs)


def fold_kernel(stage, at, *refs):
    first, second = pair_of(refs[:-2])
    keep, give = refs[-2:]
    rows = keep.shape[1] - PAD
    bit = (at[3] >> stage) % 2
    for half in range(2):
        sums = get_sums(first, (half,)) + get_sums(second, (half,))
        for out, part in ((keep, bit), (give, 1 - bit)):
            where = pl.ds(pl.multiple_of(part * rows, 16), rows)
            out[half, :rows, :] = (first[half, where, :].astype(F32) + second[half, where, :].astype(F32)).astype(BF16)
            put_sums(out, (half,), sums)


def fold_call(at, stage, operands):
    length, width = operands[0].shape[-2:]
    shape = like(2, (length - PAD) // 2 + PAD, width)
    return call(functools.partial(fold_kernel, stage), "fold_terms", (at,), operands, [shape, shape])


def part_kernel(at, *refs):
    first, second = pair_of(refs[:-2])
    rows = refs[-1].shape[1] - PAD
    for out, half in ((refs[-2], at[1]), (refs[-1], 1 - at[1])):
        out[0, :rows, :] = (first[half, :rows, :].astype(F32) + second[half, :rows, :].astype(F32)).astype(BF16)
        put_sums(out, (0,), get_sums(first, (half,)) + get_sums(second, (half,)))


def part_call(at, operands):
    length, width = operands[0].shape[-2:]
    return call(part_kernel, "part_terms", (at,), operands, [like(1, length, width)] * 2)


def share_kernel(at, mine, theirs, share, sums):
    rows = share.shape[0]
    share[...] = (mine[0, :rows, :].astype(F32) + theirs[0, :rows, :].astype(F32)).astype(BF16)
    sums[...] = get_sums(mine, (0,)) + get_sums(theirs, (0,))


def share_call(at, mine, theirs):
    one, length, width = mine.shape
    return call(
        share_kernel, "share_terms", (at,), (mine, theirs), [like(length - PAD, width), like(1, width, dtype=F32)]
    )


def join_kernel(stage, at, mine, theirs, out):
    rows = mine.shape[0]
    bit = (at[3] >> stage) % 2
    for copy in range(out.shape[0]):
        out[copy, pl.ds(pl.multiple_of(bit * rows, 16), rows), :] = mine[...]
        out[copy, pl.ds(pl.multiple_of((1 - bit) * rows, 16), rows), :] = theirs[...]


def join_call(at, stage, mine, theirs, copies):
    rows, width = mine.shape
    return call(
        functools.partial(join_kernel, stage), "join_halves", (at,), (mine, theirs), [like(copies, 2 * rows, width)]
    )[0]


def place_kernel(runs, at, *refs):
    out = refs[-1]
    for run, mine, theirs in zip(runs, refs[0:-1:2], refs[1:-1:2]):
        rows = mine.shape[0] // len(run)
        for index, entry in enumerate(run):
            low, high = units_of(entry)
            part = slice(index * rows, (index + 1) * rows)
            own = low + at[1] * (high - low)
            out[pl.ds(pl.multiple_of(own * rows, LANES), rows), :] = mine[part, :]
            out[pl.ds(pl.multiple_of((low + high - own) * rows, LANES), rows), :] = theirs[0, part, :]


def place_call(at, runs, pairs):
    rows, width = pairs[0][0].shape
    specs = [spec for mine, _ in pairs for spec in (fixed(*mine.shape), fixed(1, *mine.shape))]
    return call(
        functools.partial(place_kernel, runs),
        "place_rows",
        (at,),
        [o for pair in pairs for o in pair],
        [pltpu.HBM((rows // len(runs[0]) * UNITS, width), BF16)],
        in_specs=specs,
        us=3,
    )[0]


def spread_kernel(runs, final, at, *refs):
    units = 2 * sum(map(len, runs))
    counts, backs, refs = refs[:units], refs[units : units + 4 * len(runs)], refs[units + 4 * len(runs) :]
    scaled = refs[-1]
    step = pl.program_id(0)

    @pl.when(step == 0)
    def _():
        at_unit = 0
        for number, run in enumerate(runs):
            level, near, far, cross = backs[4 * number : 4 * number + 4]
            rows = level.shape[0] // len(run)
            for index in range(len(run)):
                part = slice(index * rows, (index + 1) * rows)
                scaled[at_unit + at[1]] = (level[part, :].astype(F32) + far[part, :].astype(F32)).astype(BF16)
                scaled[at_unit + 1 - at[1]] = (near[1, part, :].astype(F32) + cross[part, :].astype(F32)).astype(BF16)
                at_unit += 2

    total = refs[0][...] if final else None
    for index, block in enumerate(counts):
        term = lax.dot_general(block[...], scaled[index], (((0,), (0,)), ((), ())), preferred_element_type=F32)
        total = term if total is None else total + term
    out = refs[3] if final else refs[0]
    out[...] = total.astype(out.dtype)
    if final:
        mine, output, near = refs[1], refs[4], backs[1]
        half = pl.num_programs(0) // 2

        @pl.when(step // half == at[1])
        def _():
            output[...] = mine[...]

        @pl.when(step // half != at[1])
        def _():
            output[...] = near[0]


def spread_call(at, runs, counts, backs, *last):
    nodes = counts.shape[0]
    width = backs[0].shape[1]
    tile = 1024
    final = len(last) > 0
    unit_rows = nodes // UNITS
    units = [unit for run in runs for entry in run for unit in units_of(entry)]
    tiled = pl.BlockSpec((tile, width), lambda i, s: (i, 0))
    operands = [counts] * len(units) + [*backs, *last]
    specs = [pl.BlockSpec((unit_rows, tile), lambda i, s, unit=unit: (unit, i)) for unit in units]
    specs += [fixed(*o.shape) for o in backs]
    shapes, outs, aliases = [like(nodes, width, dtype=F32)], [tiled], {}
    if final:
        (low, high), steps = units, nodes // tile
        specs += [tiled, fixed(unit_rows, width), ANY]
        shapes = [pltpu.HBM((nodes, width), BF16), pltpu.HBM((nodes, width), BF16)]
        outs.append(pl.BlockSpec((unit_rows, width), lambda i, s: (jnp.where(i < steps // 2, low, high), 0)))
        aliases = {len(operands) - 1: 1}
    return call(
        functools.partial(spread_kernel, runs, final),
        "spread_back",
        (at,),
        operands,
        shapes,
        in_specs=specs,
        out_specs=outs,
        grid=(nodes // tile,),
        scratch=[pltpu.VMEM((len(units), unit_rows, width), BF16)],
        aliases=aliases,
        us=8,
    )


def tie(value, *after):
    return lax.optimization_barrier((value, *after))[0]


def local(features, neighbour_lists, node_counts, weight, bias_terms, cotangent):
    dp_count = lax.axis_size("dp")
    mp_count = lax.axis_size("mp")
    bits = dp_count.bit_length() - 1
    place = lax.axis_index("mp")
    line = lax.axis_index("dp")
    core = line % 2
    nodes, width = features.shape
    depth = weight.shape[0]
    slots = neighbour_lists.shape[1]
    live = node_counts.astype(jnp.int32)
    orders = [(low, high) for low, high in zip(range(1, bits), range(bits - 1, 0, -1))] + [(0, 0)]
    piece_rows = depth // dp_count
    piece = jnp.int32(0)
    for stage, (low, high) in enumerate(orders):
        piece = piece + (jnp.where(core == 0, line >> low, line >> high) % 2 << stage)
    at = jnp.stack([place, place % 2, core, piece]).astype(jnp.int32)

    def across(value, code):
        return lax.ppermute(value, "mp", [(i, i ^ code) for i in range(mp_count)])

    def swap(value, stage):
        pairs = []
        for i in range(dp_count):
            bit = 1 << orders[stage][i % 2]
            if not i & bit:
                pairs.append([i, i | bit])
        return lax.all_to_all(value, "dp", 0, 0, axis_index_groups=pairs)

    def along(value, stage):
        return lax.ppermute(value, "dp", [(i, i ^ (1 << orders[stage][i % 2])) for i in range(dp_count)])

    def join_pieces(value, first):
        for stage in range(bits - 1):
            last = stage == bits - 2
            came = along(value, stage)
            if stage == 0:
                came = tie(came, first)
            value = join_call(at, stage, value, came, 2 if last else 1)
            value = value if last else value[0]
        return swap(value, bits - 1).reshape(-1, width)

    unit = nodes // UNITS
    packed = neighbour_lists.reshape(nodes // 8, 8 * slots)
    piece_own = piece_call(at, weight, bias_terms, piece_rows)
    piece_sib = across(piece_own, 1)

    def count_slab(slab, counts):
        first, length = slab
        return count_call(tie(at, piece_own), packed, features, cotangent, first * unit, length * unit, counts)

    def zeros_for(function):
        return lambda *operands: jax.tree.map(
            lambda shape: jnp.zeros(shape.shape, shape.dtype), jax.eval_shape(function, *operands)
        )

    def always(function, *operands):
        return lax.cond(live[0] > 0, function, zeros_for(function), *operands)

    def last_rows(piece, counts):
        last = count_slab(SLABS[1], counts)
        return join_pieces(piece[:piece_rows], last[1]), last

    counts, *first = count_slab(SLABS[0], None)
    same, other, pack, scale = (tie(value, piece_sib) for value in first)
    parts, scales = [(same, across(pack, 1), across(same, 2), across(other, 3))], [scale]
    weight_sib, (counts, same, other, pack, scale) = always(last_rows, piece_sib, counts)
    near, far, cross = parts[0][1:]
    parts.append(
        (same, across(tie(pack, cross), 1), across(tie(same, near), 2), across(tie(other, far), 3))
    )
    scales.append(scale)

    sides = []
    for run in RUNS:
        buffers = None
        for index, entry in enumerate(run):
            buffers = row_call(
                at, live, parts[entry[0]], scales[entry[0]], cotangent, weight, weight_sib, piece_own, piece_sib,
                entry, index, len(run), buffers,
            )
        sides.append(buffers)
    grads = [side[1] for side in sides]

    def fold_terms(parts, grads):
        pair = (swap(product_call(at, parts, grads), bits - 1),)
        for stage in range(bits - 2, -1, -1):
            keep, give = fold_call(at, stage, pair)
            pair = (keep, along(give, stage))
        return part_call(at, pair)

    def share_terms(mine, theirs, counts, backs, outs):
        share, bias_grad = share_call(at, mine, theirs)
        output = place_call(at, RUNS[:-1], [(out, back[1]) for out, back in zip(outs, backs)])
        partial = spread_call(at, RUNS[:-1], counts, [o for back in backs for o in back])[0]
        return join_pieces(share, output).astype(F32), bias_grad, partial, output

    backs = []
    for index, (_, _, level, near, far, cross) in enumerate(sides):
        if index == 0:
            far, cross, near = tie(far, parts[-1][2]), tie(cross, parts[-1][3]), tie(near, parts[-1][2])
        if index == 1:
            terms = always(fold_terms, parts, [tie(grad, *backs[0][1:]) for grad in grads])
            near = tie(near, *backs[0][1:], grads[-1])
        if index == 2:
            mine, theirs = terms
            theirs = tie(theirs, *backs[0][1:], *backs[1][1:])
            came = across(theirs, 1)
            near, far, cross = tie(near, came), tie(far, theirs), tie(cross, theirs)
        backs.append((level, across(near, 1), across(far, 2), across(cross, 3)))
    outs = [side[0] for side in sides]
    weight_grad, bias_grad, partial, output = always(share_terms, mine, came, counts, backs[:-1], outs[:-1])
    features_grad, output = spread_call(at, RUNS[-1:], counts, backs[-1], partial, outs[-1], output)
    return (output, features_grad, weight_grad, bias_grad.reshape(width))


def solution(mesh):
    in_specs = (P("dp", "mp"), P("dp", None), P("dp"), P(None, "mp"), P("mp"), P("dp", "mp"))
    out_specs = (P("dp", "mp"), P("dp", "mp"), P(None, "mp"), P("mp"))
    return jax.shard_map(local, mesh=mesh, in_specs=in_specs, out_specs=out_specs, check_vma=False)
```

```python
import functools

import jax
import jax.numpy as jnp
from jax import lax
from jax.experimental import pallas as pl
from jax.experimental.pallas import tpu as pltpu
from jax.sharding import PartitionSpec as P

BF16 = jnp.bfloat16
F32 = jnp.float32
UNITS = 8
SLABS = ((0, 4), (4, 4))
RUNS = (((0, 0),), ((0, 1), (1, 0)), ((1, 1),))
LANES = 128
PAD = 16
VMEM_LIMIT = 32 << 20
ANY = pl.BlockSpec(memory_space=pl.ANY)
HBM = pl.BlockSpec(memory_space=pltpu.HBM)


def like(*shape, dtype=BF16):
    return jax.ShapeDtypeStruct(shape, dtype)


def fixed(*shape):
    return pl.BlockSpec(shape, lambda *_: (0,) * len(shape))


def units_of(entry):
    slab, block = entry
    first, length = SLABS[slab]
    return first + block, first + length // 2 + block


def call(
    kernel, name, scalars, operands, out_shape, in_specs=None, out_specs=None, grid=(1,), scratch=(), aliases=None, us=0
):
    if in_specs is None:
        in_specs = [fixed(*o.shape) for o in operands]
    if out_specs is None:
        out_specs = [fixed(*o.shape) for o in out_shape]
    return pl.pallas_call(
        kernel,
        grid_spec=pltpu.PrefetchScalarGridSpec(
            num_scalar_prefetch=len(scalars), grid=grid, in_specs=in_specs, out_specs=out_specs, scratch_shapes=scratch
        ),
        out_shape=out_shape,
        compiler_params=pltpu.CompilerParams(vmem_limit_bytes=VMEM_LIMIT),
        input_output_aliases={len(scalars) + i: o for i, o in (aliases or {}).items()},
        cost_estimate=pl.CostEstimate(flops=1, bytes_accessed=max(1, us * 3000000), transcendentals=0),
        name=name,
    )(*scalars, *operands)


def piece_kernel(at, weight, bias, out, row, sems):
    rows = out.shape[0] - PAD
    copies = [
        pltpu.make_async_copy(weight.at[pl.ds(pl.multiple_of(at[3] * rows, 16), rows), :], out.at[:rows, :], sems.at[0]),
        pltpu.make_async_copy(bias, row, sems.at[1]),
    ]
    for copy in copies:
        copy.start()
    for copy in copies:
        copy.wait()
    out[rows:, :] = jnp.broadcast_to(row[...].astype(F32).reshape(1, -1), (PAD, out.shape[1])).astype(BF16)


def piece_call(at, weight, bias, rows):
    width = weight.shape[1]
    return call(
        piece_kernel,
        "weight_piece",
        (at,),
        [pltpu.with_memory_space_constraint(value, pltpu.HBM) for value in (weight, bias)],
        [like(rows + PAD, width)],
        in_specs=[HBM, HBM],
        scratch=[pltpu.VMEM((width,), BF16), pltpu.SemaphoreType.DMA((2,))],
    )[0]


def count_kernel(base, slots, at, packed_ref, feat_ref, cot_ref, *refs):
    counts_ref, same_ref, other_ref, pack_ref, scale_ref = refs[-5:]
    rows = counts_ref.shape[0]
    step = pl.program_id(0)
    steps = pl.num_programs(0)
    block = (step + at[1] * (steps // 2)) % steps
    lanes = 8 * slots
    row = lax.broadcasted_iota(jnp.int32, (LANES, lanes), 0).astype(F32).astype(BF16)
    owner = lax.broadcasted_iota(jnp.int32, (1, lanes), 1) // slots
    one, zero = jnp.ones((LANES, lanes), BF16), jnp.zeros((LANES, lanes), BF16)

    def one_hot(index):
        tile = jnp.broadcast_to(index.astype(F32), (16, lanes)).astype(BF16)
        return jnp.where(jnp.concatenate([tile] * (LANES // 16), 0) == row, one, zero)

    def group(index):
        entry = packed_ref[index : index + 1, :]
        left = one_hot((entry >> 7) * 8 + owner)
        right = one_hot(entry & (LANES - 1))
        return lax.dot_general(left, right, (((1,), (1,)), ((), ())), preferred_element_type=F32)

    for pair in range(rows // 16):
        first, second = group(2 * pair), group(2 * pair + 1)
        for tile in range(counts_ref.shape[1] // LANES):
            counts_ref[pair * 16 : (pair + 1) * 16, tile * LANES : (tile + 1) * LANES] = jnp.concatenate(
                [first[tile * 8 : (tile + 1) * 8], second[tile * 8 : (tile + 1) * 8]], 0
            ).astype(BF16)
    degree = jnp.sum(counts_ref[...].astype(F32), axis=1, keepdims=True)
    scale = 1.0 / (degree + 1.0)
    down = lax.broadcasted_iota(jnp.int32, (LANES, LANES), 0)
    across = lax.broadcasted_iota(jnp.int32, (LANES, LANES), 1)
    twice = jnp.where(down == across, 2.0, 0.0)
    for low in range(0, rows, LANES):
        where = slice(low, low + LANES), pl.ds(pl.multiple_of(base + block * rows + low, LANES), LANES)
        counts_ref[where] = (counts_ref[where].astype(F32) + twice).astype(BF16)
    total = jnp.dot(counts_ref[...], feat_ref[...], preferred_element_type=F32)
    result = (total * scale).astype(BF16)

    @pl.when(step < steps // 2)
    def _():
        same_ref[...] = result
        scale_ref[...] = scale

    @pl.when(step >= steps // 2)
    def _():
        other_ref[...] = result
        pack_ref[0] = result
        pack_ref[1] = cot_ref[...]


def count_call(at, packed, features, cotangent, base, size, counts):
    nodes, width = features.shape
    slots = packed.shape[1] // 8
    rows = 2 * LANES
    steps = size // rows
    half = steps // 2

    def natural(i, s):
        return base // rows + (i + s[1] * half) % steps

    def early(i, s):
        return jnp.minimum(i, half - 1), 0

    def late(i, s):
        return jnp.maximum(i - half, 0), 0

    operands = [packed, features, cotangent]
    specs = [
        pl.BlockSpec((rows // 8, 8 * slots), lambda i, s: (natural(i, s), 0)),
        fixed(nodes, width),
        pl.BlockSpec((rows, width), lambda i, s: (natural(i, s), 0)),
    ]
    aliases = {}
    if counts is not None:
        aliases = {len(operands): 0}
        operands.append(counts)
        specs.append(ANY)
    return call(
        functools.partial(count_kernel, base, slots),
        "count_and_aggregate",
        (at,),
        operands,
        [
            like(nodes, nodes),
            like(size // 2, width),
            like(size // 2, width),
            like(2, size // 2, width),
            like(size // 2, 1, dtype=F32),
        ],
        in_specs=specs,
        out_specs=[
            pl.BlockSpec((rows, nodes), lambda i, s: (natural(i, s), 0)),
            pl.BlockSpec((rows, width), early),
            pl.BlockSpec((rows, width), late),
            pl.BlockSpec((2, rows, width), lambda i, s: (0, *late(i, s))),
            pl.BlockSpec((rows, 1), early),
        ],
        grid=(steps,),
        aliases=aliases,
    )


def row_kernel(
    units, at, live, part0, near, part2, part3, scale, cot_own, weight_own, weight_sib, bias_own, bias_sib, *refs
):
    out_own, grads, back0, back_near, back2, back3 = refs[-6:]
    rows, width = part0.shape
    place = at[0]
    slot = (units[0] + at[1] * (units[1] - units[0])) * rows + lax.broadcasted_iota(jnp.int32, (rows, width), 0)
    living = slot < live[0]
    starts = [pl.multiple_of((place ^ code) * width, LANES) for code in range(4)]
    values = []
    for half, (weight, bias, cot) in enumerate(
        ((weight_own, bias_own, cot_own[...]), (weight_sib, bias_sib, near[1]))
    ):
        linear = bias[0:1, :].astype(F32)
        for part, start in zip((part0[...], near[0], part2[...], part3[...]), starts):
            linear = linear + jnp.dot(part, weight[pl.ds(start, width), :], preferred_element_type=F32)
        sigma = 1.0 / (1.0 + jnp.exp(-linear))
        result = jnp.where(living, linear * sigma, 0.0).astype(BF16)
        if half == 0:
            out_own[...] = result
        else:
            back_near[0] = result
        slope = sigma * (1.0 + linear * (1.0 - sigma))
        value = jnp.where(living, cot.astype(F32) * slope, 0.0).astype(BF16)
        grads[at[1] if half == 0 else 1 - at[1]] = value
        values.append(value)
    for code, start in enumerate(starts):
        total = jnp.zeros((rows, width), F32)
        for weight, value in zip((weight_own, weight_sib), values):
            total = total + lax.dot_general(
                value, weight[pl.ds(start, width), :], (((1,), (1,)), ((), ())), preferred_element_type=F32
            )
        total = (total * scale[...]).astype(BF16)
        if code == 1:
            back_near[1] = total
        else:
            (back0, None, back2, back3)[code][...] = total


def row_call(
    at, live, parts, scale, cotangent, weight_own, weight_sib, piece_own, piece_sib, entry, index, length, buffers
):
    width = cotangent.shape[1]
    rows = cotangent.shape[0] // UNITS
    block, (low, high) = entry[1], units_of(entry)
    operands = [*parts, scale, cotangent, weight_own, weight_sib, piece_own, piece_sib]
    chunk = pl.BlockSpec((rows, width), lambda i, s, c: (block, 0))
    bias = pl.BlockSpec((PAD, width), lambda i, s, c: (piece_own.shape[0] // PAD - 1, 0))
    specs = [
        chunk,
        pl.BlockSpec((2, rows, width), lambda i, s, c: (0, block, 0)),
        chunk,
        chunk,
        pl.BlockSpec((rows, 1), lambda i, s, c: (block, 0)),
        pl.BlockSpec((rows, width), lambda i, s, c: (low + s[1] * (high - low), 0)),
        fixed(*weight_own.shape),
        fixed(*weight_sib.shape),
        bias,
        bias,
    ]
    shapes, outs, aliases = [], [], {}
    for number, double in enumerate((False, True, False, True, False, False)):
        if double:
            shapes.append(like(2, length * rows, width))
            outs.append(pl.BlockSpec((2, rows, width), lambda i, s, c: (0, index, 0)))
        else:
            shapes.append(like(length * rows, width))
            outs.append(pl.BlockSpec((rows, width), lambda i, s, c: (index, 0)))
        if index > 0:
            aliases[len(operands)] = number
            operands.append(buffers[number])
            specs.append(ANY)
    return call(
        functools.partial(row_kernel, (low, high)),
        "linear_and_slope",
        (at, live),
        operands,
        shapes,
        in_specs=specs,
        out_specs=outs,
        aliases=aliases,
    )


def put_sums(ref, index, value):
    high = value.astype(BF16)
    low = (value - high.astype(F32)).astype(BF16)
    row = lax.broadcasted_iota(jnp.int32, (PAD, value.shape[1]), 0)
    both = jnp.where(row == 0, high.astype(F32), jnp.where(row == 1, low.astype(F32), 0.0))
    ref[(*index, slice(ref.shape[-2] - PAD, None), slice(None))] = both.astype(BF16)


def get_sums(ref, index):
    rows = ref[(*index, slice(ref.shape[-2] - PAD, None), slice(None))]
    return jnp.sum(rows.astype(F32), axis=0, keepdims=True)


def product_kernel(at, *refs):
    refs, terms = refs[:-1], refs[-1]
    parts, grads = refs[: -len(RUNS)], refs[-len(RUNS) :]
    unit = grads[0].shape[1] // len(RUNS[0])
    runs = []
    for group, entries in enumerate(RUNS):
        for index, (slab, block) in enumerate(entries):
            runs.append((slab, slice(block * unit, (block + 1) * unit), group, slice(index * unit, (index + 1) * unit)))
    width = parts[0].shape[-1]
    for half in range(2):
        for code in range(4):
            total = jnp.zeros((width, width), F32)
            for slab, from_rows, group, to_rows in runs:
                part = parts[4 * slab + code]
                part = part[0, from_rows, :] if code == 1 else part[from_rows, :]
                total = total + lax.dot_general(
                    part, grads[group][half, to_rows, :], (((0,), (0,)), ((), ())), preferred_element_type=F32
                )
            block = at[0] ^ code
            rows = pl.ds(pl.multiple_of((block % 2) * width, LANES), width)
            terms[block // 2, half, rows, :] = total.astype(BF16)
        sums = sum(jnp.sum(grad[half].astype(F32), axis=0, keepdims=True) for grad in grads)
        for side in range(2):
            put_sums(terms, (side, half), sums)


def product_call(at, parts, grads):
    width = grads[0].shape[-1]
    operands = [p for quad in parts for p in quad] + list(grads)
    return call(product_kernel, "weight_product", (at,), operands, [like(2, 2, 2 * width + PAD, width)])[0]


def pair_of(refs):
    return [refs[0].at[0], refs[0].at[1]] if len(refs) == 1 else list(refs)


def fold_kernel(stage, at, *refs):
    first, second = pair_of(refs[:-2])
    keep, give = refs[-2:]
    rows = keep.shape[1] - PAD
    bit = (at[3] >> stage) % 2
    for half in range(2):
        sums = get_sums(first, (half,)) + get_sums(second, (half,))
        for out, part in ((keep, bit), (give, 1 - bit)):
            where = pl.ds(pl.multiple_of(part * rows, 16), rows)
            out[half, :rows, :] = (first[half, where, :].astype(F32) + second[half, where, :].astype(F32)).astype(BF16)
            put_sums(out, (half,), sums)


def fold_call(at, stage, operands):
    length, width = operands[0].shape[-2:]
    shape = like(2, (length - PAD) // 2 + PAD, width)
    return call(functools.partial(fold_kernel, stage), "fold_terms", (at,), operands, [shape, shape])


def part_kernel(at, *refs):
    first, second = pair_of(refs[:-2])
    rows = refs[-1].shape[1] - PAD
    for out, half in ((refs[-2], at[1]), (refs[-1], 1 - at[1])):
        out[0, :rows, :] = (first[half, :rows, :].astype(F32) + second[half, :rows, :].astype(F32)).astype(BF16)
        put_sums(out, (0,), get_sums(first, (half,)) + get_sums(second, (half,)))


def part_call(at, operands):
    length, width = operands[0].shape[-2:]
    return call(part_kernel, "part_terms", (at,), operands, [like(1, length, width)] * 2)


def share_kernel(at, mine, theirs, share, sums):
    rows = share.shape[0]
    share[...] = (mine[0, :rows, :].astype(F32) + theirs[0, :rows, :].astype(F32)).astype(BF16)
    sums[...] = get_sums(mine, (0,)) + get_sums(theirs, (0,))


def share_call(at, mine, theirs):
    one, length, width = mine.shape
    return call(
        share_kernel, "share_terms", (at,), (mine, theirs), [like(length - PAD, width), like(1, width, dtype=F32)]
    )


def join_kernel(stage, at, mine, theirs, out):
    rows = mine.shape[0]
    bit = (at[3] >> stage) % 2
    for copy in range(out.shape[0]):
        out[copy, pl.ds(pl.multiple_of(bit * rows, 16), rows), :] = mine[...]
        out[copy, pl.ds(pl.multiple_of((1 - bit) * rows, 16), rows), :] = theirs[...]


def join_call(at, stage, mine, theirs, copies):
    rows, width = mine.shape
    return call(
        functools.partial(join_kernel, stage), "join_halves", (at,), (mine, theirs), [like(copies, 2 * rows, width)]
    )[0]


def place_kernel(runs, at, *refs):
    out = refs[-1]
    for run, mine, theirs in zip(runs, refs[0:-1:2], refs[1:-1:2]):
        rows = mine.shape[0] // len(run)
        for index, entry in enumerate(run):
            low, high = units_of(entry)
            part = slice(index * rows, (index + 1) * rows)
            own = low + at[1] * (high - low)
            out[pl.ds(pl.multiple_of(own * rows, LANES), rows), :] = mine[part, :]
            out[pl.ds(pl.multiple_of((low + high - own) * rows, LANES), rows), :] = theirs[0, part, :]


def place_call(at, runs, pairs):
    rows, width = pairs[0][0].shape
    specs = [spec for mine, _ in pairs for spec in (fixed(*mine.shape), fixed(1, *mine.shape))]
    return call(
        functools.partial(place_kernel, runs),
        "place_rows",
        (at,),
        [o for pair in pairs for o in pair],
        [pltpu.HBM((rows // len(runs[0]) * UNITS, width), BF16)],
        in_specs=specs,
        us=3,
    )[0]


def spread_kernel(runs, final, at, *refs):
    units = 2 * sum(map(len, runs))
    counts, backs, refs = refs[:units], refs[units : units + 4 * len(runs)], refs[units + 4 * len(runs) :]
    scaled = refs[-1]
    step = pl.program_id(0)

    @pl.when(step == 0)
    def _():
        at_unit = 0
        for number, run in enumerate(runs):
            level, near, far, cross = backs[4 * number : 4 * number + 4]
            rows = level.shape[0] // len(run)
            for index in range(len(run)):
                part = slice(index * rows, (index + 1) * rows)
                scaled[at_unit + at[1]] = (level[part, :].astype(F32) + far[part, :].astype(F32)).astype(BF16)
                scaled[at_unit + 1 - at[1]] = (near[1, part, :].astype(F32) + cross[part, :].astype(F32)).astype(BF16)
                at_unit += 2

    total = refs[0][...] if final else None
    for index, block in enumerate(counts):
        term = lax.dot_general(block[...], scaled[index], (((0,), (0,)), ((), ())), preferred_element_type=F32)
        total = term if total is None else total + term
    out = refs[3] if final else refs[0]
    out[...] = total.astype(out.dtype)
    if final:
        mine, output, near = refs[1], refs[4], backs[1]
        half = pl.num_programs(0) // 2

        @pl.when(step // half == at[1])
        def _():
            output[...] = mine[...]

        @pl.when(step // half != at[1])
        def _():
            output[...] = near[0]


def spread_call(at, runs, counts, backs, *last):
    nodes = counts.shape[0]
    width = backs[0].shape[1]
    tile = 1024
    final = len(last) > 0
    unit_rows = nodes // UNITS
    units = [unit for run in runs for entry in run for unit in units_of(entry)]
    tiled = pl.BlockSpec((tile, width), lambda i, s: (i, 0))
    operands = [counts] * len(units) + [*backs, *last]
    specs = [pl.BlockSpec((unit_rows, tile), lambda i, s, unit=unit: (unit, i)) for unit in units]
    specs += [fixed(*o.shape) for o in backs]
    shapes, outs, aliases = [like(nodes, width, dtype=F32)], [tiled], {}
    if final:
        (low, high), steps = units, nodes // tile
        specs += [tiled, fixed(unit_rows, width), ANY]
        shapes = [pltpu.HBM((nodes, width), BF16), pltpu.HBM((nodes, width), BF16)]
        outs.append(pl.BlockSpec((unit_rows, width), lambda i, s: (jnp.where(i < steps // 2, low, high), 0)))
        aliases = {len(operands) - 1: 1}
    return call(
        functools.partial(spread_kernel, runs, final),
        "spread_back",
        (at,),
        operands,
        shapes,
        in_specs=specs,
        out_specs=outs,
        grid=(nodes // tile,),
        scratch=[pltpu.VMEM((len(units), unit_rows, width), BF16)],
        aliases=aliases,
        us=8,
    )


def tie(value, *after):
    return lax.optimization_barrier((value, *after))[0]


def local(features, neighbour_lists, node_counts, weight, bias_terms, cotangent):
    dp_count = lax.axis_size("dp")
    mp_count = lax.axis_size("mp")
    bits = dp_count.bit_length() - 1
    place = lax.axis_index("mp")
    line = lax.axis_index("dp")
    core = line % 2
    nodes, width = features.shape
    depth = weight.shape[0]
    slots = neighbour_lists.shape[1]
    live = node_counts.astype(jnp.int32)
    orders = [(low, high) for low, high in zip(range(1, bits), range(bits - 1, 0, -1))] + [(0, 0)]
    piece_rows = depth // dp_count
    piece = jnp.int32(0)
    for stage, (low, high) in enumerate(orders):
        piece = piece + (jnp.where(core == 0, line >> low, line >> high) % 2 << stage)
    at = jnp.stack([place, place % 2, core, piece]).astype(jnp.int32)

    def across(value, code):
        return lax.ppermute(value, "mp", [(i, i ^ code) for i in range(mp_count)])

    def swap(value, stage):
        pairs = []
        for i in range(dp_count):
            bit = 1 << orders[stage][i % 2]
            if not i & bit:
                pairs.append([i, i | bit])
        return lax.all_to_all(value, "dp", 0, 0, axis_index_groups=pairs)

    def along(value, stage):
        return lax.ppermute(value, "dp", [(i, i ^ (1 << orders[stage][i % 2])) for i in range(dp_count)])

    def join_pieces(value, first):
        for stage in range(bits - 1):
            last = stage == bits - 2
            came = along(value, stage)
            if stage == 0:
                came = tie(came, first)
            value = join_call(at, stage, value, came, 2 if last else 1)
            value = value if last else value[0]
        return swap(value, bits - 1).reshape(-1, width)

    unit = nodes // UNITS
    packed = neighbour_lists.reshape(nodes // 8, 8 * slots)
    piece_own = piece_call(at, weight, bias_terms, piece_rows)
    piece_sib = across(piece_own, 1)

    def count_slab(slab, counts):
        first, length = slab
        return count_call(tie(at, piece_own), packed, features, cotangent, first * unit, length * unit, counts)

    def zeros_for(function):
        return lambda *operands: jax.tree.map(
            lambda shape: jnp.zeros(shape.shape, shape.dtype), jax.eval_shape(function, *operands)
        )

    def always(function, *operands):
        return lax.cond(live[0] > 0, function, zeros_for(function), *operands)

    def last_rows(piece, counts):
        last = count_slab(SLABS[1], counts)
        return join_pieces(piece[:piece_rows], last[1]), last

    counts, *first = count_slab(SLABS[0], None)
    same, other, pack, scale = (tie(value, piece_sib) for value in first)
    parts, scales = [(same, across(pack, 1), across(same, 2), across(other, 3))], [scale]
    weight_sib, (counts, same, other, pack, scale) = always(last_rows, piece_sib, counts)
    near, far, cross = parts[0][1:]
    parts.append(
        (same, across(tie(pack, cross), 1), across(tie(same, far), 2), across(tie(other, near), 3))
    )
    scales.append(scale)

    sides = []
    for run in RUNS:
        buffers = None
        for index, entry in enumerate(run):
            buffers = row_call(
                at, live, parts[entry[0]], scales[entry[0]], cotangent, weight, weight_sib, piece_own, piece_sib,
                entry, index, len(run), buffers,
            )
        sides.append(buffers)
    grads = [side[1] for side in sides]

    def fold_terms(parts, grads):
        pair = (swap(product_call(at, parts, grads), bits - 1),)
        for stage in range(bits - 2, -1, -1):
            keep, give = fold_call(at, stage, pair)
            pair = (keep, along(give, stage))
        return part_call(at, pair)

    def share_terms(mine, theirs, counts, backs, outs):
        share, bias_grad = share_call(at, mine, theirs)
        output = place_call(at, RUNS[:-1], [(out, back[1]) for out, back in zip(outs, backs)])
        partial = spread_call(at, RUNS[:-1], counts, [o for back in backs for o in back])[0]
        return join_pieces(share, output).astype(F32), bias_grad, partial, output

    backs = []
    for index, (_, _, level, near, far, cross) in enumerate(sides):
        if index == 0:
            far, cross, near = tie(far, parts[-1][2]), tie(cross, parts[-1][3]), tie(near, parts[-1][2])
        if index == 1:
            terms = always(fold_terms, parts, [tie(grad, *backs[0][1:]) for grad in grads])
            near = tie(near, *backs[0][1:], grads[-1])
        if index == 2:
            mine, theirs = terms
            theirs = tie(theirs, *backs[0][1:], *backs[1][1:])
            came = across(theirs, 1)
            near, far, cross = tie(near, came), tie(far, theirs), tie(cross, theirs)
        backs.append((level, across(near, 1), across(far, 2), across(cross, 3)))
    outs = [side[0] for side in sides]
    weight_grad, bias_grad, partial, output = always(share_terms, mine, came, counts, backs[:-1], outs[:-1])
    features_grad, output = spread_call(at, RUNS[-1:], counts, backs[-1], partial, outs[-1], output)
    return (output, features_grad, weight_grad, bias_grad.reshape(width))


def solution(mesh):
    in_specs = (P("dp", "mp"), P("dp", None), P("dp"), P(None, "mp"), P("mp"), P("dp", "mp"))
    out_specs = (P("dp", "mp"), P("dp", "mp"), P(None, "mp"), P("mp"))
    return jax.shard_map(local, mesh=mesh, in_specs=in_specs, out_specs=out_specs, check_vma=False)
```

```python
import functools

import jax
import jax.numpy as jnp
from jax import lax
from jax.experimental import pallas as pl
from jax.experimental.pallas import tpu as pltpu
from jax.sharding import PartitionSpec as P

BF16 = jnp.bfloat16
F32 = jnp.float32
UNITS = 8
SLABS = ((0, 4), (4, 4))
RUNS = (((0, 0),), ((0, 1), (1, 0)), ((1, 1),))
LANES = 128
PAD = 16
VMEM_LIMIT = 32 << 20
ANY = pl.BlockSpec(memory_space=pl.ANY)
HBM = pl.BlockSpec(memory_space=pltpu.HBM)


def like(*shape, dtype=BF16):
    return jax.ShapeDtypeStruct(shape, dtype)


def fixed(*shape):
    return pl.BlockSpec(shape, lambda *_: (0,) * len(shape))


def units_of(entry):
    slab, block = entry
    first, length = SLABS[slab]
    return first + block, first + length // 2 + block


def call(
    kernel, name, scalars, operands, out_shape, in_specs=None, out_specs=None, grid=(1,), scratch=(), aliases=None, us=0
):
    if in_specs is None:
        in_specs = [fixed(*o.shape) for o in operands]
    if out_specs is None:
        out_specs = [fixed(*o.shape) for o in out_shape]
    return pl.pallas_call(
        kernel,
        grid_spec=pltpu.PrefetchScalarGridSpec(
            num_scalar_prefetch=len(scalars), grid=grid, in_specs=in_specs, out_specs=out_specs, scratch_shapes=scratch
        ),
        out_shape=out_shape,
        compiler_params=pltpu.CompilerParams(vmem_limit_bytes=VMEM_LIMIT),
        input_output_aliases={len(scalars) + i: o for i, o in (aliases or {}).items()},
        cost_estimate=pl.CostEstimate(flops=1, bytes_accessed=max(1, us * 3000000), transcendentals=0),
        name=name,
    )(*scalars, *operands)


def piece_kernel(at, weight, bias, out, row, sems):
    rows = out.shape[0] - PAD
    copies = [
        pltpu.make_async_copy(weight.at[pl.ds(pl.multiple_of(at[3] * rows, 16), rows), :], out.at[:rows, :], sems.at[0]),
        pltpu.make_async_copy(bias, row, sems.at[1]),
    ]
    for copy in copies:
        copy.start()
    for copy in copies:
        copy.wait()
    out[rows:, :] = jnp.broadcast_to(row[...].astype(F32).reshape(1, -1), (PAD, out.shape[1])).astype(BF16)


def piece_call(at, weight, bias, rows):
    width = weight.shape[1]
    return call(
        piece_kernel,
        "weight_piece",
        (at,),
        [pltpu.with_memory_space_constraint(value, pltpu.HBM) for value in (weight, bias)],
        [like(rows + PAD, width)],
        in_specs=[HBM, HBM],
        scratch=[pltpu.VMEM((width,), BF16), pltpu.SemaphoreType.DMA((2,))],
    )[0]


def count_kernel(base, slots, at, packed_ref, feat_ref, cot_ref, *refs):
    counts_ref, same_ref, other_ref, pack_ref, scale_ref = refs[-5:]
    rows = counts_ref.shape[0]
    step = pl.program_id(0)
    steps = pl.num_programs(0)
    block = (step + at[1] * (steps // 2)) % steps
    lanes = 8 * slots
    row = lax.broadcasted_iota(jnp.int32, (LANES, lanes), 0).astype(F32).astype(BF16)
    owner = lax.broadcasted_iota(jnp.int32, (1, lanes), 1) // slots
    one, zero = jnp.ones((LANES, lanes), BF16), jnp.zeros((LANES, lanes), BF16)

    def one_hot(index):
        tile = jnp.broadcast_to(index.astype(F32), (16, lanes)).astype(BF16)
        return jnp.where(jnp.concatenate([tile] * (LANES // 16), 0) == row, one, zero)

    def group(index):
        entry = packed_ref[index : index + 1, :]
        left = one_hot((entry >> 7) * 8 + owner)
        right = one_hot(entry & (LANES - 1))
        return lax.dot_general(left, right, (((1,), (1,)), ((), ())), preferred_element_type=F32)

    for pair in range(rows // 16):
        first, second = group(2 * pair), group(2 * pair + 1)
        for tile in range(counts_ref.shape[1] // LANES):
            counts_ref[pair * 16 : (pair + 1) * 16, tile * LANES : (tile + 1) * LANES] = jnp.concatenate(
                [first[tile * 8 : (tile + 1) * 8], second[tile * 8 : (tile + 1) * 8]], 0
            ).astype(BF16)
    degree = jnp.sum(counts_ref[...].astype(F32), axis=1, keepdims=True)
    scale = 1.0 / (degree + 1.0)
    down = lax.broadcasted_iota(jnp.int32, (LANES, LANES), 0)
    across = lax.broadcasted_iota(jnp.int32, (LANES, LANES), 1)
    twice = jnp.where(down == across, 2.0, 0.0)
    for low in range(0, rows, LANES):
        where = slice(low, low + LANES), pl.ds(pl.multiple_of(base + block * rows + low, LANES), LANES)
        counts_ref[where] = (counts_ref[where].astype(F32) + twice).astype(BF16)
    total = jnp.dot(counts_ref[...], feat_ref[...], preferred_element_type=F32)
    result = (total * scale).astype(BF16)

    @pl.when(step < steps // 2)
    def _():
        same_ref[...] = result
        scale_ref[...] = scale

    @pl.when(step >= steps // 2)
    def _():
        other_ref[...] = result
        pack_ref[0] = result
        pack_ref[1] = cot_ref[...]


def count_call(at, packed, features, cotangent, base, size, counts):
    nodes, width = features.shape
    slots = packed.shape[1] // 8
    rows = 4 * LANES
    steps = size // rows
    half = steps // 2

    def natural(i, s):
        return base // rows + (i + s[1] * half) % steps

    def early(i, s):
        return jnp.minimum(i, half - 1), 0

    def late(i, s):
        return jnp.maximum(i - half, 0), 0

    operands = [packed, features, cotangent]
    specs = [
        pl.BlockSpec((rows // 8, 8 * slots), lambda i, s: (natural(i, s), 0)),
        fixed(nodes, width),
        pl.BlockSpec((rows, width), lambda i, s: (natural(i, s), 0)),
    ]
    aliases = {}
    if counts is not None:
        aliases = {len(operands): 0}
        operands.append(counts)
        specs.append(ANY)
    return call(
        functools.partial(count_kernel, base, slots),
        "count_and_aggregate",
        (at,),
        operands,
        [
            like(nodes, nodes),
            like(size // 2, width),
            like(size // 2, width),
            like(2, size // 2, width),
            like(size // 2, 1, dtype=F32),
        ],
        in_specs=specs,
        out_specs=[
            pl.BlockSpec((rows, nodes), lambda i, s: (natural(i, s), 0)),
            pl.BlockSpec((rows, width), early),
            pl.BlockSpec((rows, width), late),
            pl.BlockSpec((2, rows, width), lambda i, s: (0, *late(i, s))),
            pl.BlockSpec((rows, 1), early),
        ],
        grid=(steps,),
        aliases=aliases,
    )


def row_kernel(
    units, at, live, part0, near, part2, part3, scale, cot_own, weight_own, weight_sib, bias_own, bias_sib, *refs
):
    out_own, grads, back0, back_near, back2, back3 = refs[-6:]
    rows, width = part0.shape
    place = at[0]
    slot = (units[0] + at[1] * (units[1] - units[0])) * rows + lax.broadcasted_iota(jnp.int32, (rows, width), 0)
    living = slot < live[0]
    starts = [pl.multiple_of((place ^ code) * width, LANES) for code in range(4)]
    values = []
    for half, (weight, bias, cot) in enumerate(
        ((weight_own, bias_own, cot_own[...]), (weight_sib, bias_sib, near[1]))
    ):
        linear = bias[0:1, :].astype(F32)
        for part, start in zip((part0[...], near[0], part2[...], part3[...]), starts):
            linear = linear + jnp.dot(part, weight[pl.ds(start, width), :], preferred_element_type=F32)
        sigma = 1.0 / (1.0 + jnp.exp(-linear))
        result = jnp.where(living, linear * sigma, 0.0).astype(BF16)
        if half == 0:
            out_own[...] = result
        else:
            back_near[0] = result
        slope = sigma * (1.0 + linear * (1.0 - sigma))
        value = jnp.where(living, cot.astype(F32) * slope, 0.0).astype(BF16)
        grads[at[1] if half == 0 else 1 - at[1]] = value
        values.append(value)
    for code, start in enumerate(starts):
        total = jnp.zeros((rows, width), F32)
        for weight, value in zip((weight_own, weight_sib), values):
            total = total + lax.dot_general(
                value, weight[pl.ds(start, width), :], (((1,), (1,)), ((), ())), preferred_element_type=F32
            )
        total = (total * scale[...]).astype(BF16)
        if code == 1:
            back_near[1] = total
        else:
            (back0, None, back2, back3)[code][...] = total


def row_call(
    at, live, parts, scale, cotangent, weight_own, weight_sib, piece_own, piece_sib, entry, index, length, buffers
):
    width = cotangent.shape[1]
    rows = cotangent.shape[0] // UNITS
    block, (low, high) = entry[1], units_of(entry)
    operands = [*parts, scale, cotangent, weight_own, weight_sib, piece_own, piece_sib]
    chunk = pl.BlockSpec((rows, width), lambda i, s, c: (block, 0))
    bias = pl.BlockSpec((PAD, width), lambda i, s, c: (piece_own.shape[0] // PAD - 1, 0))
    specs = [
        chunk,
        pl.BlockSpec((2, rows, width), lambda i, s, c: (0, block, 0)),
        chunk,
        chunk,
        pl.BlockSpec((rows, 1), lambda i, s, c: (block, 0)),
        pl.BlockSpec((rows, width), lambda i, s, c: (low + s[1] * (high - low), 0)),
        fixed(*weight_own.shape),
        fixed(*weight_sib.shape),
        bias,
        bias,
    ]
    shapes, outs, aliases = [], [], {}
    for number, double in enumerate((False, True, False, True, False, False)):
        if double:
            shapes.append(like(2, length * rows, width))
            outs.append(pl.BlockSpec((2, rows, width), lambda i, s, c: (0, index, 0)))
        else:
            shapes.append(like(length * rows, width))
            outs.append(pl.BlockSpec((rows, width), lambda i, s, c: (index, 0)))
        if index > 0:
            aliases[len(operands)] = number
            operands.append(buffers[number])
            specs.append(ANY)
    return call(
        functools.partial(row_kernel, (low, high)),
        "linear_and_slope",
        (at, live),
        operands,
        shapes,
        in_specs=specs,
        out_specs=outs,
        aliases=aliases,
    )


def put_sums(ref, index, value):
    high = value.astype(BF16)
    low = (value - high.astype(F32)).astype(BF16)
    row = lax.broadcasted_iota(jnp.int32, (PAD, value.shape[1]), 0)
    both = jnp.where(row == 0, high.astype(F32), jnp.where(row == 1, low.astype(F32), 0.0))
    ref[(*index, slice(ref.shape[-2] - PAD, None), slice(None))] = both.astype(BF16)


def get_sums(ref, index):
    rows = ref[(*index, slice(ref.shape[-2] - PAD, None), slice(None))]
    return jnp.sum(rows.astype(F32), axis=0, keepdims=True)


def product_kernel(at, *refs):
    refs, terms = refs[:-1], refs[-1]
    parts, grads = refs[: -len(RUNS)], refs[-len(RUNS) :]
    unit = grads[0].shape[1] // len(RUNS[0])
    runs = []
    for group, entries in enumerate(RUNS):
        for index, (slab, block) in enumerate(entries):
            runs.append((slab, slice(block * unit, (block + 1) * unit), group, slice(index * unit, (index + 1) * unit)))
    width = parts[0].shape[-1]
    for half in range(2):
        for code in range(4):
            total = jnp.zeros((width, width), F32)
            for slab, from_rows, group, to_rows in runs:
                part = parts[4 * slab + code]
                part = part[0, from_rows, :] if code == 1 else part[from_rows, :]
                total = total + lax.dot_general(
                    part, grads[group][half, to_rows, :], (((0,), (0,)), ((), ())), preferred_element_type=F32
                )
            block = at[0] ^ code
            rows = pl.ds(pl.multiple_of((block % 2) * width, LANES), width)
            terms[block // 2, half, rows, :] = total.astype(BF16)
        sums = sum(jnp.sum(grad[half].astype(F32), axis=0, keepdims=True) for grad in grads)
        for side in range(2):
            put_sums(terms, (side, half), sums)


def product_call(at, parts, grads):
    width = grads[0].shape[-1]
    operands = [p for quad in parts for p in quad] + list(grads)
    return call(product_kernel, "weight_product", (at,), operands, [like(2, 2, 2 * width + PAD, width)])[0]


def pair_of(refs):
    return [refs[0].at[0], refs[0].at[1]] if len(refs) == 1 else list(refs)


def fold_kernel(stage, at, *refs):
    first, second = pair_of(refs[:-2])
    keep, give = refs[-2:]
    rows = keep.shape[1] - PAD
    bit = (at[3] >> stage) % 2
    for half in range(2):
        sums = get_sums(first, (half,)) + get_sums(second, (half,))
        for out, part in ((keep, bit), (give, 1 - bit)):
            where = pl.ds(pl.multiple_of(part * rows, 16), rows)
            out[half, :rows, :] = (first[half, where, :].astype(F32) + second[half, where, :].astype(F32)).astype(BF16)
            put_sums(out, (half,), sums)


def fold_call(at, stage, operands):
    length, width = operands[0].shape[-2:]
    shape = like(2, (length - PAD) // 2 + PAD, width)
    return call(functools.partial(fold_kernel, stage), "fold_terms", (at,), operands, [shape, shape])


def part_kernel(at, *refs):
    first, second = pair_of(refs[:-2])
    rows = refs[-1].shape[1] - PAD
    for out, half in ((refs[-2], at[1]), (refs[-1], 1 - at[1])):
        out[0, :rows, :] = (first[half, :rows, :].astype(F32) + second[half, :rows, :].astype(F32)).astype(BF16)
        put_sums(out, (0,), get_sums(first, (half,)) + get_sums(second, (half,)))


def part_call(at, operands):
    length, width = operands[0].shape[-2:]
    return call(part_kernel, "part_terms", (at,), operands, [like(1, length, width)] * 2)


def share_kernel(at, mine, theirs, share, sums):
    rows = share.shape[0]
    share[...] = (mine[0, :rows, :].astype(F32) + theirs[0, :rows, :].astype(F32)).astype(BF16)
    sums[...] = get_sums(mine, (0,)) + get_sums(theirs, (0,))


def share_call(at, mine, theirs):
    one, length, width = mine.shape
    return call(
        share_kernel, "share_terms", (at,), (mine, theirs), [like(length - PAD, width), like(1, width, dtype=F32)]
    )


def join_kernel(stage, at, mine, theirs, out):
    rows = mine.shape[0]
    bit = (at[3] >> stage) % 2
    for copy in range(out.shape[0]):
        out[copy, pl.ds(pl.multiple_of(bit * rows, 16), rows), :] = mine[...]
        out[copy, pl.ds(pl.multiple_of((1 - bit) * rows, 16), rows), :] = theirs[...]


def join_call(at, stage, mine, theirs, copies):
    rows, width = mine.shape
    return call(
        functools.partial(join_kernel, stage), "join_halves", (at,), (mine, theirs), [like(copies, 2 * rows, width)]
    )[0]


def place_kernel(runs, at, *refs):
    out = refs[-1]
    for run, mine, theirs in zip(runs, refs[0:-1:2], refs[1:-1:2]):
        rows = mine.shape[0] // len(run)
        for index, entry in enumerate(run):
            low, high = units_of(entry)
            part = slice(index * rows, (index + 1) * rows)
            own = low + at[1] * (high - low)
            out[pl.ds(pl.multiple_of(own * rows, LANES), rows), :] = mine[part, :]
            out[pl.ds(pl.multiple_of((low + high - own) * rows, LANES), rows), :] = theirs[0, part, :]


def place_call(at, runs, pairs):
    rows, width = pairs[0][0].shape
    specs = [spec for mine, _ in pairs for spec in (fixed(*mine.shape), fixed(1, *mine.shape))]
    return call(
        functools.partial(place_kernel, runs),
        "place_rows",
        (at,),
        [o for pair in pairs for o in pair],
        [pltpu.HBM((rows // len(runs[0]) * UNITS, width), BF16)],
        in_specs=specs,
        us=3,
    )[0]


def spread_kernel(runs, final, at, *refs):
    units = 2 * sum(map(len, runs))
    counts, backs, refs = refs[:units], refs[units : units + 4 * len(runs)], refs[units + 4 * len(runs) :]
    scaled = refs[-1]
    step = pl.program_id(0)

    @pl.when(step == 0)
    def _():
        at_unit = 0
        for number, run in enumerate(runs):
            level, near, far, cross = backs[4 * number : 4 * number + 4]
            rows = level.shape[0] // len(run)
            for index in range(len(run)):
                part = slice(index * rows, (index + 1) * rows)
                scaled[at_unit + at[1]] = (level[part, :].astype(F32) + far[part, :].astype(F32)).astype(BF16)
                scaled[at_unit + 1 - at[1]] = (near[1, part, :].astype(F32) + cross[part, :].astype(F32)).astype(BF16)
                at_unit += 2

    total = refs[0][...] if final else None
    for index, block in enumerate(counts):
        term = lax.dot_general(block[...], scaled[index], (((0,), (0,)), ((), ())), preferred_element_type=F32)
        total = term if total is None else total + term
    out = refs[3] if final else refs[0]
    out[...] = total.astype(out.dtype)
    if final:
        mine, output, near = refs[1], refs[4], backs[1]
        half = pl.num_programs(0) // 2

        @pl.when(step // half == at[1])
        def _():
            output[...] = mine[...]

        @pl.when(step // half != at[1])
        def _():
            output[...] = near[0]


def spread_call(at, runs, counts, backs, *last):
    nodes = counts.shape[0]
    width = backs[0].shape[1]
    tile = 1024
    final = len(last) > 0
    unit_rows = nodes // UNITS
    units = [unit for run in runs for entry in run for unit in units_of(entry)]
    tiled = pl.BlockSpec((tile, width), lambda i, s: (i, 0))
    operands = [counts] * len(units) + [*backs, *last]
    specs = [pl.BlockSpec((unit_rows, tile), lambda i, s, unit=unit: (unit, i)) for unit in units]
    specs += [fixed(*o.shape) for o in backs]
    shapes, outs, aliases = [like(nodes, width, dtype=F32)], [tiled], {}
    if final:
        (low, high), steps = units, nodes // tile
        specs += [tiled, fixed(unit_rows, width), ANY]
        shapes = [pltpu.HBM((nodes, width), BF16), pltpu.HBM((nodes, width), BF16)]
        outs.append(pl.BlockSpec((unit_rows, width), lambda i, s: (jnp.where(i < steps // 2, low, high), 0)))
        aliases = {len(operands) - 1: 1}
    return call(
        functools.partial(spread_kernel, runs, final),
        "spread_back",
        (at,),
        operands,
        shapes,
        in_specs=specs,
        out_specs=outs,
        grid=(nodes // tile,),
        scratch=[pltpu.VMEM((len(units), unit_rows, width), BF16)],
        aliases=aliases,
        us=8,
    )


def tie(value, *after):
    return lax.optimization_barrier((value, *after))[0]


def local(features, neighbour_lists, node_counts, weight, bias_terms, cotangent):
    dp_count = lax.axis_size("dp")
    mp_count = lax.axis_size("mp")
    bits = dp_count.bit_length() - 1
    place = lax.axis_index("mp")
    line = lax.axis_index("dp")
    core = line % 2
    nodes, width = features.shape
    depth = weight.shape[0]
    slots = neighbour_lists.shape[1]
    live = node_counts.astype(jnp.int32)
    orders = [(low, high) for low, high in zip(range(1, bits), range(bits - 1, 0, -1))] + [(0, 0)]
    piece_rows = depth // dp_count
    piece = jnp.int32(0)
    for stage, (low, high) in enumerate(orders):
        piece = piece + (jnp.where(core == 0, line >> low, line >> high) % 2 << stage)
    at = jnp.stack([place, place % 2, core, piece]).astype(jnp.int32)

    def across(value, code):
        return lax.ppermute(value, "mp", [(i, i ^ code) for i in range(mp_count)])

    def swap(value, stage):
        pairs = []
        for i in range(dp_count):
            bit = 1 << orders[stage][i % 2]
            if not i & bit:
                pairs.append([i, i | bit])
        return lax.all_to_all(value, "dp", 0, 0, axis_index_groups=pairs)

    def along(value, stage):
        return lax.ppermute(value, "dp", [(i, i ^ (1 << orders[stage][i % 2])) for i in range(dp_count)])

    def join_pieces(value, first):
        for stage in range(bits - 1):
            last = stage == bits - 2
            came = along(value, stage)
            if stage == 0:
                came = tie(came, first)
            value = join_call(at, stage, value, came, 2 if last else 1)
            value = value if last else value[0]
        return swap(value, bits - 1).reshape(-1, width)

    unit = nodes // UNITS
    packed = neighbour_lists.reshape(nodes // 8, 8 * slots)
    piece_own = piece_call(at, weight, bias_terms, piece_rows)
    piece_sib = across(piece_own, 1)

    def count_slab(slab, counts):
        first, length = slab
        return count_call(tie(at, piece_own), packed, features, cotangent, first * unit, length * unit, counts)

    def zeros_for(function):
        return lambda *operands: jax.tree.map(
            lambda shape: jnp.zeros(shape.shape, shape.dtype), jax.eval_shape(function, *operands)
        )

    def always(function, *operands):
        return lax.cond(live[0] > 0, function, zeros_for(function), *operands)

    def last_rows(piece, counts):
        last = count_slab(SLABS[1], counts)
        return join_pieces(piece[:piece_rows], last[1]), last

    counts, *first = count_slab(SLABS[0], None)
    same, other, pack, scale = (tie(value, piece_sib) for value in first)
    parts, scales = [(same, across(pack, 1), across(same, 2), across(other, 3))], [scale]
    weight_sib, (counts, same, other, pack, scale) = always(last_rows, piece_sib, counts)
    near, far, cross = parts[0][1:]
    parts.append(
        (same, across(tie(pack, cross), 1), across(tie(same, far), 2), across(tie(other, near), 3))
    )
    scales.append(scale)

    sides = []
    for run in RUNS:
        buffers = None
        for index, entry in enumerate(run):
            buffers = row_call(
                at, live, parts[entry[0]], scales[entry[0]], cotangent, weight, weight_sib, piece_own, piece_sib,
                entry, index, len(run), buffers,
            )
        sides.append(buffers)
    grads = [side[1] for side in sides]

    def fold_terms(parts, grads):
        pair = (swap(product_call(at, parts, grads), bits - 1),)
        for stage in range(bits - 2, -1, -1):
            keep, give = fold_call(at, stage, pair)
            pair = (keep, along(give, stage))
        return part_call(at, pair)

    def share_terms(mine, theirs, counts, backs, outs):
        share, bias_grad = share_call(at, mine, theirs)
        output = place_call(at, RUNS[:-1], [(out, back[1]) for out, back in zip(outs, backs)])
        partial = spread_call(at, RUNS[:-1], counts, [o for back in backs for o in back])[0]
        return join_pieces(share, output).astype(F32), bias_grad, partial, output

    backs = []
    for index, (_, _, level, near, far, cross) in enumerate(sides):
        if index == 0:
            far, cross, near = tie(far, parts[-1][2]), tie(cross, parts[-1][3]), tie(near, parts[-1][3])
        if index == 1:
            terms = always(fold_terms, parts, [tie(grad, *backs[0][1:]) for grad in grads])
            near = tie(near, *backs[0][1:], grads[-1])
        if index == 2:
            mine, theirs = terms
            theirs = tie(theirs, *backs[0][1:], *backs[1][1:])
            came = across(theirs, 1)
            near, far, cross = tie(near, came), tie(far, theirs), tie(cross, theirs)
        backs.append((level, across(near, 1), across(far, 2), across(cross, 3)))
    outs = [side[0] for side in sides]
    weight_grad, bias_grad, partial, output = always(share_terms, mine, came, counts, backs[:-1], outs[:-1])
    features_grad, output = spread_call(at, RUNS[-1:], counts, backs[-1], partial, outs[-1], output)
    return (output, features_grad, weight_grad, bias_grad.reshape(width))


def solution(mesh):
    in_specs = (P("dp", "mp"), P("dp", None), P("dp"), P(None, "mp"), P("mp"), P("dp", "mp"))
    out_specs = (P("dp", "mp"), P("dp", "mp"), P(None, "mp"), P("mp"))
    return jax.shard_map(local, mesh=mesh, in_specs=in_specs, out_specs=out_specs, check_vma=False)
```

```python
import functools

import jax
import jax.numpy as jnp
from jax import lax
from jax.experimental import pallas as pl
from jax.experimental.pallas import tpu as pltpu
from jax.sharding import PartitionSpec as P

BF16 = jnp.bfloat16
F32 = jnp.float32
UNITS = 8
SLABS = ((0, 4), (4, 4))
RUNS = (((0, 0),), ((0, 1), (1, 0)), ((1, 1),))
LANES = 128
PAD = 16
VMEM_LIMIT = 32 << 20
ANY = pl.BlockSpec(memory_space=pl.ANY)
HBM = pl.BlockSpec(memory_space=pltpu.HBM)


def like(*shape, dtype=BF16):
    return jax.ShapeDtypeStruct(shape, dtype)


def fixed(*shape):
    return pl.BlockSpec(shape, lambda *_: (0,) * len(shape))


def units_of(entry):
    slab, block = entry
    first, length = SLABS[slab]
    return first + block, first + length // 2 + block


def call(
    kernel, name, scalars, operands, out_shape, in_specs=None, out_specs=None, grid=(1,), scratch=(), aliases=None, us=0
):
    if in_specs is None:
        in_specs = [fixed(*o.shape) for o in operands]
    if out_specs is None:
        out_specs = [fixed(*o.shape) for o in out_shape]
    return pl.pallas_call(
        kernel,
        grid_spec=pltpu.PrefetchScalarGridSpec(
            num_scalar_prefetch=len(scalars), grid=grid, in_specs=in_specs, out_specs=out_specs, scratch_shapes=scratch
        ),
        out_shape=out_shape,
        compiler_params=pltpu.CompilerParams(vmem_limit_bytes=VMEM_LIMIT),
        input_output_aliases={len(scalars) + i: o for i, o in (aliases or {}).items()},
        cost_estimate=pl.CostEstimate(flops=1, bytes_accessed=max(1, us * 3000000), transcendentals=0),
        name=name,
    )(*scalars, *operands)


def piece_kernel(at, weight, bias, out, row, sems):
    rows = out.shape[0] - PAD
    copies = [
        pltpu.make_async_copy(weight.at[pl.ds(pl.multiple_of(at[3] * rows, 16), rows), :], out.at[:rows, :], sems.at[0]),
        pltpu.make_async_copy(bias, row, sems.at[1]),
    ]
    for copy in copies:
        copy.start()
    for copy in copies:
        copy.wait()
    out[rows:, :] = jnp.broadcast_to(row[...].astype(F32).reshape(1, -1), (PAD, out.shape[1])).astype(BF16)


def piece_call(at, weight, bias, rows):
    width = weight.shape[1]
    return call(
        piece_kernel,
        "weight_piece",
        (at,),
        [pltpu.with_memory_space_constraint(value, pltpu.HBM) for value in (weight, bias)],
        [like(rows + PAD, width)],
        in_specs=[HBM, HBM],
        scratch=[pltpu.VMEM((width,), BF16), pltpu.SemaphoreType.DMA((2,))],
    )[0]


def count_kernel(base, slots, at, packed_ref, feat_ref, cot_ref, *refs):
    counts_ref, same_ref, other_ref, pack_ref, scale_ref = refs[-5:]
    rows = counts_ref.shape[0]
    step = pl.program_id(0)
    steps = pl.num_programs(0)
    block = (step + at[1] * (steps // 2)) % steps
    lanes = 8 * slots
    row = lax.broadcasted_iota(jnp.int32, (LANES, lanes), 0).astype(F32).astype(BF16)
    owner = lax.broadcasted_iota(jnp.int32, (1, lanes), 1) // slots
    one, zero = jnp.ones((LANES, lanes), BF16), jnp.zeros((LANES, lanes), BF16)

    def one_hot(index):
        tile = jnp.broadcast_to(index.astype(F32), (16, lanes)).astype(BF16)
        return jnp.where(jnp.concatenate([tile] * (LANES // 16), 0) == row, one, zero)

    def group(index):
        entry = packed_ref[index : index + 1, :]
        left = one_hot((entry >> 7) * 8 + owner)
        right = one_hot(entry & (LANES - 1))
        return lax.dot_general(left, right, (((1,), (1,)), ((), ())), preferred_element_type=F32)

    for pair in range(rows // 16):
        first, second = group(2 * pair), group(2 * pair + 1)
        for tile in range(counts_ref.shape[1] // LANES):
            counts_ref[pair * 16 : (pair + 1) * 16, tile * LANES : (tile + 1) * LANES] = jnp.concatenate(
                [first[tile * 8 : (tile + 1) * 8], second[tile * 8 : (tile + 1) * 8]], 0
            ).astype(BF16)
    degree = jnp.sum(counts_ref[...].astype(F32), axis=1, keepdims=True)
    scale = 1.0 / (degree + 1.0)
    down = lax.broadcasted_iota(jnp.int32, (LANES, LANES), 0)
    across = lax.broadcasted_iota(jnp.int32, (LANES, LANES), 1)
    twice = jnp.where(down == across, 2.0, 0.0)
    for low in range(0, rows, LANES):
        where = slice(low, low + LANES), pl.ds(pl.multiple_of(base + block * rows + low, LANES), LANES)
        counts_ref[where] = (counts_ref[where].astype(F32) + twice).astype(BF16)
    total = jnp.dot(counts_ref[...], feat_ref[...], preferred_element_type=F32)
    result = (total * scale).astype(BF16)

    @pl.when(step < steps // 2)
    def _():
        same_ref[...] = result
        scale_ref[...] = scale

    @pl.when(step >= steps // 2)
    def _():
        other_ref[...] = result
        pack_ref[0] = result
        pack_ref[1] = cot_ref[...]


def count_call(at, packed, features, cotangent, base, size, counts):
    nodes, width = features.shape
    slots = packed.shape[1] // 8
    rows = 4 * LANES
    steps = size // rows
    half = steps // 2

    def natural(i, s):
        return base // rows + (i + s[1] * half) % steps

    def early(i, s):
        return jnp.minimum(i, half - 1), 0

    def late(i, s):
        return jnp.maximum(i - half, 0), 0

    operands = [packed, features, cotangent]
    specs = [
        pl.BlockSpec((rows // 8, 8 * slots), lambda i, s: (natural(i, s), 0)),
        fixed(nodes, width),
        pl.BlockSpec((rows, width), lambda i, s: (natural(i, s), 0)),
    ]
    aliases = {}
    if counts is not None:
        aliases = {len(operands): 0}
        operands.append(counts)
        specs.append(ANY)
    return call(
        functools.partial(count_kernel, base, slots),
        "count_and_aggregate",
        (at,),
        operands,
        [
            like(nodes, nodes),
            like(size // 2, width),
            like(size // 2, width),
            like(2, size // 2, width),
            like(size // 2, 1, dtype=F32),
        ],
        in_specs=specs,
        out_specs=[
            pl.BlockSpec((rows, nodes), lambda i, s: (natural(i, s), 0)),
            pl.BlockSpec((rows, width), early),
            pl.BlockSpec((rows, width), late),
            pl.BlockSpec((2, rows, width), lambda i, s: (0, *late(i, s))),
            pl.BlockSpec((rows, 1), early),
        ],
        grid=(steps,),
        aliases=aliases,
    )


def row_kernel(
    units, at, live, part0, near, part2, part3, scale, cot_own, weight_own, weight_sib, bias_own, bias_sib, *refs
):
    out_own, grads, back0, back_near, back2, back3 = refs[-6:]
    rows, width = part0.shape
    place = at[0]
    slot = (units[0] + at[1] * (units[1] - units[0])) * rows + lax.broadcasted_iota(jnp.int32, (rows, width), 0)
    living = slot < live[0]
    starts = [pl.multiple_of((place ^ code) * width, LANES) for code in range(4)]
    values = []
    for half, (weight, bias, cot) in enumerate(
        ((weight_own, bias_own, cot_own[...]), (weight_sib, bias_sib, near[1]))
    ):
        linear = bias[0:1, :].astype(F32)
        for part, start in zip((part0[...], near[0], part2[...], part3[...]), starts):
            linear = linear + jnp.dot(part, weight[pl.ds(start, width), :], preferred_element_type=F32)
        sigma = 1.0 / (1.0 + jnp.exp(-linear))
        result = jnp.where(living, linear * sigma, 0.0).astype(BF16)
        if half == 0:
            out_own[...] = result
        else:
            back_near[0] = result
        slope = sigma * (1.0 + linear * (1.0 - sigma))
        value = jnp.where(living, cot.astype(F32) * slope, 0.0).astype(BF16)
        grads[at[1] if half == 0 else 1 - at[1]] = value
        values.append(value)
    for code, start in enumerate(starts):
        total = jnp.zeros((rows, width), F32)
        for weight, value in zip((weight_own, weight_sib), values):
            total = total + lax.dot_general(
                value, weight[pl.ds(start, width), :], (((1,), (1,)), ((), ())), preferred_element_type=F32
            )
        total = (total * scale[...]).astype(BF16)
        if code == 1:
            back_near[1] = total
        else:
            (back0, None, back2, back3)[code][...] = total


def row_call(
    at, live, parts, scale, cotangent, weight_own, weight_sib, piece_own, piece_sib, entry, index, length, buffers
):
    width = cotangent.shape[1]
    rows = cotangent.shape[0] // UNITS
    block, (low, high) = entry[1], units_of(entry)
    operands = [*parts, scale, cotangent, weight_own, weight_sib, piece_own, piece_sib]
    chunk = pl.BlockSpec((rows, width), lambda i, s, c: (block, 0))
    bias = pl.BlockSpec((PAD, width), lambda i, s, c: (piece_own.shape[0] // PAD - 1, 0))
    specs = [
        chunk,
        pl.BlockSpec((2, rows, width), lambda i, s, c: (0, block, 0)),
        chunk,
        chunk,
        pl.BlockSpec((rows, 1), lambda i, s, c: (block, 0)),
        pl.BlockSpec((rows, width), lambda i, s, c: (low + s[1] * (high - low), 0)),
        fixed(*weight_own.shape),
        fixed(*weight_sib.shape),
        bias,
        bias,
    ]
    shapes, outs, aliases = [], [], {}
    for number, double in enumerate((False, True, False, True, False, False)):
        if double:
            shapes.append(like(2, length * rows, width))
            outs.append(pl.BlockSpec((2, rows, width), lambda i, s, c: (0, index, 0)))
        else:
            shapes.append(like(length * rows, width))
            outs.append(pl.BlockSpec((rows, width), lambda i, s, c: (index, 0)))
        if index > 0:
            aliases[len(operands)] = number
            operands.append(buffers[number])
            specs.append(ANY)
    return call(
        functools.partial(row_kernel, (low, high)),
        "linear_and_slope",
        (at, live),
        operands,
        shapes,
        in_specs=specs,
        out_specs=outs,
        aliases=aliases,
    )


def put_sums(ref, index, value):
    high = value.astype(BF16)
    low = (value - high.astype(F32)).astype(BF16)
    row = lax.broadcasted_iota(jnp.int32, (PAD, value.shape[1]), 0)
    both = jnp.where(row == 0, high.astype(F32), jnp.where(row == 1, low.astype(F32), 0.0))
    ref[(*index, slice(ref.shape[-2] - PAD, None), slice(None))] = both.astype(BF16)


def get_sums(ref, index):
    rows = ref[(*index, slice(ref.shape[-2] - PAD, None), slice(None))]
    return jnp.sum(rows.astype(F32), axis=0, keepdims=True)


def product_kernel(at, *refs):
    refs, terms = refs[:-1], refs[-1]
    parts, grads = refs[: -len(RUNS)], refs[-len(RUNS) :]
    unit = grads[0].shape[1] // len(RUNS[0])
    runs = []
    for group, entries in enumerate(RUNS):
        for index, (slab, block) in enumerate(entries):
            runs.append((slab, slice(block * unit, (block + 1) * unit), group, slice(index * unit, (index + 1) * unit)))
    width = parts[0].shape[-1]
    for half in range(2):
        for code in range(4):
            total = jnp.zeros((width, width), F32)
            for slab, from_rows, group, to_rows in runs:
                part = parts[4 * slab + code]
                part = part[0, from_rows, :] if code == 1 else part[from_rows, :]
                total = total + lax.dot_general(
                    part, grads[group][half, to_rows, :], (((0,), (0,)), ((), ())), preferred_element_type=F32
                )
            block = at[0] ^ code
            rows = pl.ds(pl.multiple_of((block % 2) * width, LANES), width)
            terms[block // 2, half, rows, :] = total.astype(BF16)
        sums = sum(jnp.sum(grad[half].astype(F32), axis=0, keepdims=True) for grad in grads)
        for side in range(2):
            put_sums(terms, (side, half), sums)


def product_call(at, parts, grads):
    width = grads[0].shape[-1]
    operands = [p for quad in parts for p in quad] + list(grads)
    return call(product_kernel, "weight_product", (at,), operands, [like(2, 2, 2 * width + PAD, width)])[0]


def pair_of(refs):
    return [refs[0].at[0], refs[0].at[1]] if len(refs) == 1 else list(refs)


def fold_kernel(stage, at, *refs):
    first, second = pair_of(refs[:-2])
    keep, give = refs[-2:]
    rows = keep.shape[1] - PAD
    bit = (at[3] >> stage) % 2
    for half in range(2):
        sums = get_sums(first, (half,)) + get_sums(second, (half,))
        for out, part in ((keep, bit), (give, 1 - bit)):
            where = pl.ds(pl.multiple_of(part * rows, 16), rows)
            out[half, :rows, :] = (first[half, where, :].astype(F32) + second[half, where, :].astype(F32)).astype(BF16)
            put_sums(out, (half,), sums)


def fold_call(at, stage, operands):
    length, width = operands[0].shape[-2:]
    shape = like(2, (length - PAD) // 2 + PAD, width)
    return call(functools.partial(fold_kernel, stage), "fold_terms", (at,), operands, [shape, shape])


def part_kernel(at, *refs):
    first, second = pair_of(refs[:-2])
    rows = refs[-1].shape[1] - PAD
    for out, half in ((refs[-2], at[1]), (refs[-1], 1 - at[1])):
        out[0, :rows, :] = (first[half, :rows, :].astype(F32) + second[half, :rows, :].astype(F32)).astype(BF16)
        put_sums(out, (0,), get_sums(first, (half,)) + get_sums(second, (half,)))


def part_call(at, operands):
    length, width = operands[0].shape[-2:]
    return call(part_kernel, "part_terms", (at,), operands, [like(1, length, width)] * 2)


def share_kernel(at, mine, theirs, share, sums):
    rows = share.shape[0]
    share[...] = (mine[0, :rows, :].astype(F32) + theirs[0, :rows, :].astype(F32)).astype(BF16)
    sums[...] = get_sums(mine, (0,)) + get_sums(theirs, (0,))


def share_call(at, mine, theirs):
    one, length, width = mine.shape
    return call(
        share_kernel, "share_terms", (at,), (mine, theirs), [like(length - PAD, width), like(1, width, dtype=F32)]
    )


def join_kernel(stage, at, mine, theirs, out):
    rows = mine.shape[0]
    bit = (at[3] >> stage) % 2
    for copy in range(out.shape[0]):
        out[copy, pl.ds(pl.multiple_of(bit * rows, 16), rows), :] = mine[...]
        out[copy, pl.ds(pl.multiple_of((1 - bit) * rows, 16), rows), :] = theirs[...]


def join_call(at, stage, mine, theirs, copies):
    rows, width = mine.shape
    return call(
        functools.partial(join_kernel, stage), "join_halves", (at,), (mine, theirs), [like(copies, 2 * rows, width)]
    )[0]


def place_kernel(runs, at, *refs):
    out = refs[-1]
    for run, mine, theirs in zip(runs, refs[0:-1:2], refs[1:-1:2]):
        rows = mine.shape[0] // len(run)
        for index, entry in enumerate(run):
            low, high = units_of(entry)
            part = slice(index * rows, (index + 1) * rows)
            own = low + at[1] * (high - low)
            out[pl.ds(pl.multiple_of(own * rows, LANES), rows), :] = mine[part, :]
            out[pl.ds(pl.multiple_of((low + high - own) * rows, LANES), rows), :] = theirs[0, part, :]


def place_call(at, runs, pairs):
    rows, width = pairs[0][0].shape
    specs = [spec for mine, _ in pairs for spec in (fixed(*mine.shape), fixed(1, *mine.shape))]
    return call(
        functools.partial(place_kernel, runs),
        "place_rows",
        (at,),
        [o for pair in pairs for o in pair],
        [pltpu.HBM((rows // len(runs[0]) * UNITS, width), BF16)],
        in_specs=specs,
        us=3,
    )[0]


def spread_kernel(runs, final, at, *refs):
    units = 2 * sum(map(len, runs))
    counts, backs, refs = refs[:units], refs[units : units + 4 * len(runs)], refs[units + 4 * len(runs) :]
    scaled = refs[-1]
    step = pl.program_id(0)

    @pl.when(step == 0)
    def _():
        at_unit = 0
        for number, run in enumerate(runs):
            level, near, far, cross = backs[4 * number : 4 * number + 4]
            rows = level.shape[0] // len(run)
            for index in range(len(run)):
                part = slice(index * rows, (index + 1) * rows)
                scaled[at_unit + at[1]] = (level[part, :].astype(F32) + far[part, :].astype(F32)).astype(BF16)
                scaled[at_unit + 1 - at[1]] = (near[1, part, :].astype(F32) + cross[part, :].astype(F32)).astype(BF16)
                at_unit += 2

    total = refs[0][...] if final else None
    for index, block in enumerate(counts):
        term = lax.dot_general(block[...], scaled[index], (((0,), (0,)), ((), ())), preferred_element_type=F32)
        total = term if total is None else total + term
    out = refs[3] if final else refs[0]
    out[...] = total.astype(out.dtype)
    if final:
        mine, output, near = refs[1], refs[4], backs[1]
        half = pl.num_programs(0) // 2

        @pl.when(step // half == at[1])
        def _():
            output[...] = mine[...]

        @pl.when(step // half != at[1])
        def _():
            output[...] = near[0]


def spread_call(at, runs, counts, backs, *last):
    nodes = counts.shape[0]
    width = backs[0].shape[1]
    tile = 1024
    final = len(last) > 0
    unit_rows = nodes // UNITS
    units = [unit for run in runs for entry in run for unit in units_of(entry)]
    tiled = pl.BlockSpec((tile, width), lambda i, s: (i, 0))
    operands = [counts] * len(units) + [*backs, *last]
    specs = [pl.BlockSpec((unit_rows, tile), lambda i, s, unit=unit: (unit, i)) for unit in units]
    specs += [fixed(*o.shape) for o in backs]
    shapes, outs, aliases = [like(nodes, width, dtype=F32)], [tiled], {}
    if final:
        (low, high), steps = units, nodes // tile
        specs += [tiled, fixed(unit_rows, width), ANY]
        shapes = [pltpu.HBM((nodes, width), BF16), pltpu.HBM((nodes, width), BF16)]
        outs.append(pl.BlockSpec((unit_rows, width), lambda i, s: (jnp.where(i < steps // 2, low, high), 0)))
        aliases = {len(operands) - 1: 1}
    return call(
        functools.partial(spread_kernel, runs, final),
        "spread_back",
        (at,),
        operands,
        shapes,
        in_specs=specs,
        out_specs=outs,
        grid=(nodes // tile,),
        scratch=[pltpu.VMEM((len(units), unit_rows, width), BF16)],
        aliases=aliases,
        us=8,
    )


def tie(value, *after):
    return lax.optimization_barrier((value, *after))[0]


def local(features, neighbour_lists, node_counts, weight, bias_terms, cotangent):
    dp_count = lax.axis_size("dp")
    mp_count = lax.axis_size("mp")
    bits = dp_count.bit_length() - 1
    place = lax.axis_index("mp")
    line = lax.axis_index("dp")
    core = line % 2
    nodes, width = features.shape
    depth = weight.shape[0]
    slots = neighbour_lists.shape[1]
    live = node_counts.astype(jnp.int32)
    orders = [(low, high) for low, high in zip(range(1, bits), range(bits - 1, 0, -1))] + [(0, 0)]
    piece_rows = depth // dp_count
    piece = jnp.int32(0)
    for stage, (low, high) in enumerate(orders):
        piece = piece + (jnp.where(core == 0, line >> low, line >> high) % 2 << stage)
    at = jnp.stack([place, place % 2, core, piece]).astype(jnp.int32)

    def across(value, code):
        return lax.ppermute(value, "mp", [(i, i ^ code) for i in range(mp_count)])

    def swap(value, stage):
        pairs = []
        for i in range(dp_count):
            bit = 1 << orders[stage][i % 2]
            if not i & bit:
                pairs.append([i, i | bit])
        return lax.all_to_all(value, "dp", 0, 0, axis_index_groups=pairs)

    def along(value, stage):
        return lax.ppermute(value, "dp", [(i, i ^ (1 << orders[stage][i % 2])) for i in range(dp_count)])

    def join_pieces(value, first):
        for stage in range(bits - 1):
            last = stage == bits - 2
            came = along(value, stage)
            if stage == 0:
                came = tie(came, first)
            value = join_call(at, stage, value, came, 2 if last else 1)
            value = value if last else value[0]
        return swap(value, bits - 1).reshape(-1, width)

    unit = nodes // UNITS
    packed = neighbour_lists.reshape(nodes // 8, 8 * slots)
    piece_own = piece_call(at, weight, bias_terms, piece_rows)
    piece_sib = across(piece_own, 1)

    def count_slab(slab, counts):
        first, length = slab
        return count_call(tie(at, piece_own), packed, features, cotangent, first * unit, length * unit, counts)

    def zeros_for(function):
        return lambda *operands: jax.tree.map(
            lambda shape: jnp.zeros(shape.shape, shape.dtype), jax.eval_shape(function, *operands)
        )

    def always(function, *operands):
        return lax.cond(live[0] > 0, function, zeros_for(function), *operands)

    def last_rows(piece, counts):
        last = count_slab(SLABS[1], counts)
        return join_pieces(piece[:piece_rows], last[1]), last

    counts, *first = count_slab(SLABS[0], None)
    same, other, pack, scale = (tie(value, piece_sib) for value in first)
    parts, scales = [(same, across(pack, 1), across(same, 2), across(other, 3))], [scale]
    weight_sib, (counts, same, other, pack, scale) = always(last_rows, piece_sib, counts)
    near, far, cross = parts[0][1:]
    parts.append(
        (same, across(tie(pack, cross), 1), across(tie(same, far), 2), across(tie(other, near), 3))
    )
    scales.append(scale)

    sides = []
    for run in RUNS:
        buffers = None
        for index, entry in enumerate(run):
            buffers = row_call(
                at, live, parts[entry[0]], scales[entry[0]], cotangent, weight, weight_sib, piece_own, piece_sib,
                entry, index, len(run), buffers,
            )
        sides.append(buffers)
    grads = [side[1] for side in sides]

    def fold_terms(parts, grads):
        pair = (swap(product_call(at, parts, grads), bits - 1),)
        for stage in range(bits - 2, -1, -1):
            keep, give = fold_call(at, stage, pair)
            pair = (keep, along(give, stage))
        return part_call(at, pair)

    def share_terms(share, counts, backs, outs):
        output = place_call(at, RUNS[:-1], [(out, back[1]) for out, back in zip(outs, backs)])
        partial = spread_call(at, RUNS[:-1], counts, [o for back in backs for o in back])[0]
        return join_pieces(share, output).astype(F32), partial, output

    backs = []
    for index, (_, _, level, near, far, cross) in enumerate(sides):
        if index == 0:
            far, cross, near = tie(far, parts[-1][2]), tie(cross, parts[-1][3]), tie(near, parts[-1][3])
        if index == 1:
            terms = always(fold_terms, parts, [tie(grad, *backs[0][1:]) for grad in grads])
            near = tie(near, *backs[0][1:], grads[-1])
        if index == 2:
            mine, theirs = terms
            theirs = tie(theirs, *backs[0][1:], *backs[1][1:])
            came = across(theirs, 1)
            near, far, cross = tie(near, came), tie(far, theirs), tie(cross, theirs)
        backs.append((level, across(near, 1), across(far, 2), across(cross, 3)))
    outs = [side[0] for side in sides]
    share, bias_grad = share_call(at, mine, came)
    weight_grad, partial, output = always(share_terms, share, counts, backs[:-1], outs[:-1])
    features_grad, output = spread_call(at, RUNS[-1:], counts, backs[-1], partial, outs[-1], output)
    return (output, features_grad, weight_grad, bias_grad.reshape(width))


def solution(mesh):
    in_specs = (P("dp", "mp"), P("dp", None), P("dp"), P(None, "mp"), P("mp"), P("dp", "mp"))
    out_specs = (P("dp", "mp"), P("dp", "mp"), P(None, "mp"), P("mp"))
    return jax.shard_map(local, mesh=mesh, in_specs=in_specs, out_specs=out_specs, check_vma=False)
```
